512 devices in a mesh: dp: 2 (over core), section: 8 (over z), mp: 32 (over x, y).
Axes of the slice: x: 4, y: 8, z: 8, core: 2. Of those that a mesh axis runs over, the one named last changes fastest.
Arguments:
- activations: bfloat16 [2, 8, 128, 128, 384], P('dp', 'section', 'mp'), may hold values from -8 to 8
- out_grads: bfloat16 [2, 8, 128, 128, 384], P('dp', 'section', 'mp'), may hold values from -6 to 6
- layer_weights: bfloat16 [8, 4, 384, 384], P('section'), may hold values from -1.5 to 1.5
Outputs:
- received: bfloat16 [2, 8, 128, 128, 384], P('dp', 'section', 'mp')
- weight_grads: float32 [8, 4, 384, 384], P('section', 'dp', 'mp')
The draws below stay inside these ranges and needn't reach their ends.
All inputs are finite; a program needn't handle non-finite values.
Results may differ from the reference program's by a relative error of at most 0.011.
Values may be sent and summed in bfloat16 or wider, within the bound.
No kernel may reach another device: no remote copies, remote signals or barrier semaphores. Data moves between devices by JAX's collectives and lax.ppermute only.
A program may use at most 64 MiB of HBM per device.

```python
import jax
import jax.numpy as jnp
from jax import lax

D = 384
HEADS = 6
HEAD_DIM = 64
SEQS = 128
RES = 128
N_DP = 2
N_SECTION = 8


def draw_activations(key, part):
    shape = (N_DP, N_SECTION, SEQS, RES, D)
    first = jax.random.fold_in(key, 0)
    base = jax.random.normal(first, shape, jnp.float32)
    return jnp.clip(base, -8.0, 8.0).astype(jnp.bfloat16)


def draw_layer_weights(key, part):
    first = jax.random.fold_in(key, 0)
    base = jax.random.normal(first, (N_SECTION, 4, D, HEADS, HEAD_DIM), jnp.float32) * D ** (-0.5)
    return jnp.clip(base.reshape(N_SECTION, 4, D, HEADS * HEAD_DIM), -1.5, 1.5).astype(jnp.bfloat16)


def levels(stream_key, shape, pieces, smallest, top_value):
    factor_of = 1.0
    for position, blocks in pieces:
        draws = jax.random.uniform(jax.random.fold_in(jax.random.fold_in(stream_key, 6), position), (blocks,), jnp.float32, smallest / len(pieces), top_value / len(pieces))
        factor_of = factor_of * jnp.repeat(jnp.exp(draws), shape[position] // blocks).reshape((-1,) + (1,) * (len(shape) - 1 - position))
    return factor_of


def scatter_about(key, dims, spread, bound, shards=(), held_as=jnp.bfloat16):
    result = spread * jax.random.normal(key, dims, jnp.float32)
    if shards:
        result = result * levels(key, dims, shards, -0.22, 0.18)
    return jnp.clip(result, -bound, bound).astype(held_as)


def setup_inputs(seed: int = 0) -> dict:
    key_of = jax.random.split(jax.random.key(seed), 4)
    activations = draw_activations(jax.random.fold_in(key_of[3], 71), 0)
    out_grads = scatter_about(key_of[1], (N_DP, N_SECTION, SEQS, RES, D), 1.0, 6.0, ((0, 2), (1, 8), (2, 32)))
    layer_weights = draw_layer_weights(jax.random.fold_in(key_of[3], 71), 0)
    return {"activations": activations, "out_grads": out_grads, "layer_weights": layer_weights}


EPS = 1e-05

def widen(tensor):
    return lax.optimization_barrier(tensor).astype(jnp.float32)

def normalize(values):
    mean_value = lax.optimization_barrier(jnp.mean(values, axis=-1, keepdims=True))
    centred = values - mean_value
    inverse = lax.rsqrt(lax.optimization_barrier(jnp.mean(centred * centred, axis=-1, keepdims=True)) + EPS)
    return (centred * inverse, inverse)

def norm_backward(grad_in, standard, inverse):
    grad_mean = lax.optimization_barrier(jnp.mean(grad_in, axis=-1, keepdims=True))
    grad_proj = lax.optimization_barrier(jnp.mean(grad_in * standard, axis=-1, keepdims=True))
    return inverse * (grad_in - grad_mean - standard * grad_proj)

def one_column(operands):
    queries, key_rows, values_in, out_delta = operands
    scaling = HEAD_DIM ** (-0.5)
    scores = jnp.einsum('she,the->hst', queries, key_rows) * scaling
    row_max = lax.optimization_barrier(jnp.max(scores, axis=-1, keepdims=True))
    exponent = jnp.exp(scores - row_max)
    probs = exponent / lax.optimization_barrier(jnp.sum(exponent, axis=-1, keepdims=True))
    soft = widen(probs.astype(jnp.bfloat16))
    attn_out = jnp.einsum('hst,the->she', soft, values_in).astype(jnp.bfloat16)
    dprobs = jnp.einsum('she,the->hst', out_delta, values_in)
    row_delta = lax.optimization_barrier(jnp.sum(probs * dprobs, axis=-1, keepdims=True))
    dscores = widen((probs * (dprobs - row_delta)).astype(jnp.bfloat16))
    query_grad = (jnp.einsum('hst,the->she', dscores, key_rows) * scaling).astype(jnp.bfloat16)
    key_grad = (jnp.einsum('hst,she->the', dscores, queries) * scaling).astype(jnp.bfloat16)
    value_grad = jnp.einsum('hst,she->the', soft, out_delta).astype(jnp.bfloat16)
    return (attn_out, query_grad, key_grad, value_grad)

def section_grads(acts, grads_out, weight):
    seq_count, res_count, model_width = acts.shape
    tokens = seq_count * res_count
    head_width = weight.shape[2]
    standard, inverse = normalize(acts.reshape(tokens, model_width).astype(jnp.float32))
    normed = standard.astype(jnp.bfloat16)
    projected = [jnp.dot(normed, weight[slot_index], preferred_element_type=jnp.float32).astype(jnp.bfloat16) for slot_index in range(3)]
    out_flat = grads_out.reshape(tokens, model_width)
    attn_grad = jnp.dot(out_flat, weight[3], preferred_element_type=jnp.float32).astype(jnp.bfloat16)

    def columns(tensor):
        return widen(tensor).reshape(seq_count, res_count, HEADS, HEAD_DIM).transpose(1, 0, 2, 3)
    results = lax.map(one_column, (columns(projected[0]), columns(projected[1]), columns(projected[2]), columns(attn_grad)))

    def flatten(tensor):
        return tensor.transpose(1, 0, 2, 3).reshape(tokens, head_width)
    attn_out, query_grad, key_grad, value_grad = (flatten(tensor) for tensor in results)
    normed_grad = jnp.dot(query_grad, weight[0].T, preferred_element_type=jnp.float32)
    normed_grad = normed_grad + jnp.dot(key_grad, weight[1].T, preferred_element_type=jnp.float32)
    normed_grad = normed_grad + jnp.dot(value_grad, weight[2].T, preferred_element_type=jnp.float32)
    branch = widen(norm_backward(normed_grad, standard, inverse).astype(jnp.bfloat16))
    input_grad = (out_flat.astype(jnp.float32) + branch).astype(jnp.bfloat16).reshape(seq_count, res_count, model_width)
    grads = jnp.stack([jnp.dot(normed.T, query_grad, preferred_element_type=jnp.float32), jnp.dot(normed.T, key_grad, preferred_element_type=jnp.float32), jnp.dot(normed.T, value_grad, preferred_element_type=jnp.float32), jnp.dot(out_flat.T, attn_out, preferred_element_type=jnp.float32)])
    return (input_grad, grads)

def reference(activations, out_grads, layer_weights):
    input_rows = []
    grad_rows = []
    for replica in range(N_DP):
        section_rows = []
        for section_index in range(N_SECTION):
            input_grad, grads = section_grads(activations[replica, section_index], out_grads[replica, section_index], layer_weights[section_index])
            section_rows.append(input_grad)
            if replica == 0:
                grad_rows.append(grads)
            else:
                grad_rows[section_index] = grad_rows[section_index] + grads
        input_rows.append(section_rows)
    received_rows = []
    for replica in range(N_DP):
        shifted = []
        for section_index in range(N_SECTION):
            if section_index + 1 < N_SECTION:
                shifted.append(input_rows[replica][section_index + 1])
            else:
                shifted.append(jnp.zeros_like(input_rows[replica][section_index]))
        received_rows.append(jnp.stack(shifted))
    received = jnp.stack(received_rows)
    weight_grads = jnp.stack(grad_rows)
    return (received, weight_grads)
```

```python
import functools

import jax
import jax.numpy as jnp
from jax import lax
from jax.experimental import pallas as pl
from jax.experimental.pallas import tpu as pltpu
from jax.sharding import PartitionSpec as P

HEAD_DIM = 64
EPS = 1e-05
F32 = jnp.float32
BF16 = jnp.bfloat16
LANES = 128
ROWS = 4
COLS = 4
CELL = ROWS * COLS
GROUP = 16
BLOCK = GROUP * CELL
VMEM = pl.BlockSpec(memory_space=pltpu.VMEM)
SMEM = pl.BlockSpec(memory_space=pltpu.SMEM)


def dot(a, b, dims=((1,), (0,))):
    return lax.dot_general(a, b, (dims, ((), ())), preferred_element_type=F32)


def selection(size, source_of):
    out = lax.broadcasted_iota(jnp.int32, (size, size), 0)
    source = lax.broadcasted_iota(jnp.int32, (size, size), 1)
    return jnp.where(source_of(out) == source, 1.0, 0.0).astype(BF16)


def reorder(matrix, rows):
    return dot(matrix, rows).astype(BF16)


def pack_kernel(act_ref, grad_ref, out_ref):
    order = selection(BLOCK, lambda o: ((o >> 2) & 3) * 64 + (o >> 4) * 4 + (o & 3))
    groups = out_ref.shape[0] // GROUP
    residues = act_ref.shape[0] // ROWS
    span = GROUP * COLS
    for slot, ref in enumerate((act_ref, grad_ref)):
        for g in range(groups):
            rows = jnp.concatenate(
                [ref[i * residues + g * span : i * residues + (g + 1) * span] for i in range(ROWS)]
            )
            moved = reorder(order, rows).reshape(GROUP, CELL, -1)
            out_ref[g * GROUP : (g + 1) * GROUP, slot * CELL : (slot + 1) * CELL] = moved


def main_kernel(
    in_ref,
    weight_ref,
    back_ref,
    normed_ref,
    grads_ref,
    attn_ref,
    delta_ref,
    standard_ref,
    inverse_ref,
    proj_ref,
):
    peers = in_ref.shape[0]
    groups = peers // GROUP
    width = in_ref.shape[2]
    seqs = peers * ROWS
    tokens = seqs * COLS
    span = GROUP * ROWS
    order = selection(BLOCK, lambda o: ((o >> 2) & 15) * 16 + (o & 3) * 4 + (o >> 6))
    for g in range(groups):
        peers_of = slice(g * GROUP, (g + 1) * GROUP)
        acts = dot(order, in_ref[peers_of, :CELL].reshape(BLOCK, width))
        outs = reorder(order, in_ref[peers_of, CELL : 2 * CELL].reshape(BLOCK, width))
        for j in range(COLS):
            to = slice(j * seqs + g * span, j * seqs + (g + 1) * span)
            standard_ref[to] = acts[j * span : (j + 1) * span]
            delta_ref[to] = outs[j * span : (j + 1) * span]
    values = standard_ref[...]
    mean_value = jnp.mean(values, axis=-1, keepdims=True)
    centred = values - mean_value
    inverse = lax.rsqrt(jnp.mean(centred * centred, axis=-1, keepdims=True) + EPS)
    standard = centred * inverse
    standard_ref[...] = standard
    inverse_ref[...] = jnp.broadcast_to(inverse, inverse_ref.shape)
    normed = standard.astype(BF16)
    normed_ref[...] = normed
    for n in range(3):
        proj_ref[n] = dot(normed, weight_ref[n]).astype(BF16)
    proj_ref[3] = dot(delta_ref[...], weight_ref[3]).astype(BF16)

    scaling = HEAD_DIM ** (-0.5)
    low = lax.broadcasted_iota(jnp.int32, (seqs, LANES), 1) < HEAD_DIM

    def apart(pair):
        zero = jnp.zeros_like(pair)
        return jnp.concatenate([jnp.where(low, pair, zero), jnp.where(low, zero, pair)])

    def joined(rows):
        return jnp.where(low, rows[:seqs], rows[seqs:])

    def halves(rows, function):
        return jnp.concatenate([function(rows[:, :seqs]), function(rows[:, seqs:])], axis=1)

    def column(j, carry):
        here = pl.ds(pl.multiple_of(j * seqs, seqs), seqs)
        for pair in range(width // LANES):
            lanes = slice(pair * LANES, (pair + 1) * LANES)
            query, key, value, delta = (proj_ref[n, here, lanes] for n in range(4))
            keys, vals = apart(key), apart(value)
            scores = dot(query, keys, ((1,), (1,))) * scaling
            dprobs = dot(delta, vals, ((1,), (1,)))
            probs, soft, dscores = [], [], []
            for h in range(2):
                part = scores[:, h * seqs : (h + 1) * seqs]
                exponent = jnp.exp(part - jnp.max(part, axis=-1, keepdims=True))
                prob = exponent / jnp.sum(exponent, axis=-1, keepdims=True)
                dprob = dprobs[:, h * seqs : (h + 1) * seqs]
                row_delta = jnp.sum(prob * dprob, axis=-1, keepdims=True)
                soft.append(prob.astype(BF16))
                dscores.append((prob * (dprob - row_delta)).astype(BF16))
            soft = jnp.concatenate(soft, axis=1)
            dscores = jnp.concatenate(dscores, axis=1)
            attn_ref[here, lanes] = dot(soft, vals).astype(BF16)
            grads_ref[0, here, lanes] = (dot(dscores, keys) * scaling).astype(BF16)
            key_grad = joined(dot(dscores, query, ((0,), (0,))))
            grads_ref[1, here, lanes] = (key_grad * scaling).astype(BF16)
            grads_ref[2, here, lanes] = joined(dot(soft, delta, ((0,), (0,)))).astype(BF16)
        return carry

    lax.fori_loop(0, COLS, column, 0)

    grad_in = dot(grads_ref[0], weight_ref[0], ((1,), (1,)))
    grad_in += dot(grads_ref[1], weight_ref[1], ((1,), (1,)))
    grad_in += dot(grads_ref[2], weight_ref[2], ((1,), (1,)))
    standard = standard_ref[...]
    grad_mean = jnp.mean(grad_in, axis=-1, keepdims=True)
    grad_proj = jnp.mean(grad_in * standard, axis=-1, keepdims=True)
    branch = inverse_ref[:, :1] * (grad_in - grad_mean - standard * grad_proj)
    branch = branch.astype(BF16).astype(F32)
    input_grad = (delta_ref[...].astype(F32) + branch).astype(BF16)
    order = selection(BLOCK, lambda o: (o & 3) * 64 + (o >> 4) * 4 + ((o >> 2) & 3))
    for g in range(groups):
        rows = jnp.concatenate(
            [input_grad[j * seqs + g * span : j * seqs + (g + 1) * span] for j in range(COLS)]
        )
        back_ref[g * GROUP : (g + 1) * GROUP] = reorder(order, rows).reshape(GROUP, CELL, width)


def weight_kernel(replica_ref, normed_ref, grads_ref, attn_ref, delta_ref, keep_ref, give_ref):
    replica = replica_ref[0]
    for n in range(4):
        if n < 3:
            term = dot(normed_ref[...], grads_ref[n], ((0,), (0,)))
        else:
            term = dot(delta_ref[...], attn_ref[...], ((0,), (0,)))

        @pl.when(replica == n // 2)
        def _():
            keep_ref[n % 2] = term

        @pl.when(replica != n // 2)
        def _():
            give_ref[n % 2] = term.astype(BF16)


def combine_kernel(keep_ref, got_ref, back_ref, out_ref):
    peers, cells, width = back_ref.shape
    part = width // peers
    out_ref[:, :cells] = back_ref[...]
    size = 8 * part

    def source_of(o):
        device = o // (2 * part)
        inside = o - device * (2 * part)
        matrix = inside // part
        return matrix * size + device * part + inside - matrix * part

    order = selection(2 * size, source_of)
    for g in range(peers // 8):
        here = slice(g * size, (g + 1) * size)
        rows = [(keep_ref[m, here] + got_ref[m, here].astype(F32)).astype(BF16) for m in range(2)]
        moved = reorder(order, jnp.concatenate(rows)).reshape(8, 2 * part, width)
        out_ref[g * 8 : (g + 1) * 8, cells:] = moved


def final_kernel(in_ref, received_ref, grads_ref):
    peers, _, width = in_ref.shape
    groups = peers // GROUP
    residues = peers * COLS
    span = GROUP * COLS
    order = selection(BLOCK, lambda o: ((o >> 2) & 15) * 16 + (o >> 6) * 4 + (o & 3))
    for g in range(groups):
        rows = in_ref[g * GROUP : (g + 1) * GROUP, :CELL].reshape(BLOCK, width)
        moved = reorder(order, rows)
        for i in range(ROWS):
            to = slice(i * residues + g * span, i * residues + (g + 1) * span)
            received_ref[to] = moved[i * span : (i + 1) * span]
    grads_ref[...] = jnp.sum(in_ref[:, CELL:].astype(F32), axis=0)


def shape(dims, dtype=BF16):
    return jax.ShapeDtypeStruct(dims, dtype)


def call(kernel, in_specs, out_shape, scratch=()):
    return pl.pallas_call(
        kernel,
        in_specs=in_specs,
        out_specs=jax.tree.map(lambda _: VMEM, out_shape),
        out_shape=out_shape,
        scratch_shapes=scratch,
        compiler_params=pltpu.CompilerParams(vmem_limit_bytes=56 * 1024 * 1024),
    )


def exchange(array):
    return lax.all_to_all(array, "mp", split_axis=0, concat_axis=0, tiled=True)


def per_device(activations, out_grads, layer_weights):
    rows, residues, width = activations.shape[2:]
    peers = lax.axis_size("mp")
    tokens = rows * residues
    part = width // peers
    packed = call(pack_kernel, [VMEM] * 2, shape((peers, 2 * CELL, width)))(
        activations.reshape(tokens, width), out_grads.reshape(tokens, width)
    )
    arrived = exchange(packed)
    back, normed, grads, attn, delta = call(
        main_kernel,
        [VMEM] * 2,
        (
            shape((peers, CELL, width)),
            shape((tokens, width)),
            shape((3, tokens, width)),
            shape((tokens, width)),
            shape((tokens, width)),
        ),
        [
            pltpu.VMEM((tokens, width), F32),
            pltpu.VMEM((tokens, LANES), F32),
            pltpu.VMEM((4, tokens, width), BF16),
        ],
    )(arrived, layer_weights[0])
    sections = lax.axis_size("section")
    back = lax.ppermute(back, "section", [(i + 1, i) for i in range(sections - 1)])
    replica = lax.axis_index("dp").astype(jnp.int32).reshape(1)
    keep, give = call(
        weight_kernel,
        [SMEM] + [VMEM] * 4,
        (shape((2, width, width), F32), shape((2, width, width))),
    )(replica, normed, grads, attn, delta)
    got = lax.ppermute(give, "dp", [(0, 1), (1, 0)])
    leaving = call(combine_kernel, [VMEM] * 3, shape((peers, CELL + 2 * part, width)))(
        keep, got, back
    )
    landed = exchange(leaving)
    received, weight_grads = call(
        final_kernel, [VMEM], (shape((tokens, width)), shape((2 * part, width), F32))
    )(landed)
    return (received.reshape(activations.shape), weight_grads.reshape(1, 2, part, width))


def solution(mesh):
    in_specs = (
        P("dp", "section", "mp", None, None),
        P("dp", "section", "mp", None, None),
        P("section", None, None, None),
    )
    out_specs = (P("dp", "section", "mp", None, None), P("section", "dp", "mp", None))
    return jax.shard_map(
        per_device, mesh=mesh, in_specs=in_specs, out_specs=out_specs, check_vma=False
    )
```

```python
import jax
import jax.numpy as jnp
from jax import lax
from jax.experimental import pallas as pl
from jax.experimental.pallas import tpu as pltpu
from jax.sharding import PartitionSpec as P


HEAD_DIM = 64
EPS = 1e-05
F32 = jnp.float32
BF16 = jnp.bfloat16
LANES = 128
ROWS = 4
COLS = 4
CELL = ROWS * COLS
GROUP = 16
BLOCK = GROUP * CELL
NX = 4
PAD = 8
VMEM = pl.BlockSpec(memory_space=pltpu.VMEM)
SMEM = pl.BlockSpec(memory_space=pltpu.SMEM)


def dot(a, b, dims=((1,), (0,))):
    return lax.dot_general(a, b, (dims, ((), ())), preferred_element_type=F32)


def selection(size, source_of):
    out = lax.broadcasted_iota(jnp.int32, (size, size), 0)
    source = lax.broadcasted_iota(jnp.int32, (size, size), 1)
    return jnp.where(source_of(out) == source, 1.0, 0.0).astype(BF16)


def reorder(matrix, rows):
    return dot(matrix, rows).astype(BF16)


def pack_kernel(act_ref, grad_ref, out_ref):
    order = selection(BLOCK, lambda o: ((o >> 2) & 3) * 64 + (o >> 4) * 4 + (o & 3))
    groups = out_ref.shape[0] // GROUP
    residues = act_ref.shape[0] // ROWS
    span = GROUP * COLS
    for slot, ref in enumerate((act_ref, grad_ref)):
        for g in range(groups):
            rows = jnp.concatenate(
                [ref[i * residues + g * span : i * residues + (g + 1) * span] for i in range(ROWS)]
            )
            moved = reorder(order, rows).reshape(GROUP, CELL, -1)
            out_ref[g * GROUP : (g + 1) * GROUP, slot * CELL : (slot + 1) * CELL] = moved


def attend_kernel(
    replica_ref,
    in_ref,
    weight_ref,
    grads_ref,
    delta_ref,
    standard_ref,
    inverse_ref,
    keep_ref,
    give_ref,
    normed_ref,
    attn_ref,
    proj_ref,
):
    peers = in_ref.shape[0]
    groups = peers // GROUP
    width = in_ref.shape[2]
    seqs = peers * ROWS
    span = GROUP * ROWS
    order = selection(BLOCK, lambda o: ((o >> 2) & 15) * 16 + (o & 3) * 4 + (o >> 6))
    for g in range(groups):
        peers_of = slice(g * GROUP, (g + 1) * GROUP)
        acts = dot(order, in_ref[peers_of, :CELL].reshape(BLOCK, width))
        outs = reorder(order, in_ref[peers_of, CELL : 2 * CELL].reshape(BLOCK, width))
        for j in range(COLS):
            to = slice(j * seqs + g * span, j * seqs + (g + 1) * span)
            standard_ref[to] = acts[j * span : (j + 1) * span]
            delta_ref[to] = outs[j * span : (j + 1) * span]
    values = standard_ref[...]
    mean_value = jnp.mean(values, axis=-1, keepdims=True)
    centred = values - mean_value
    inverse = lax.rsqrt(jnp.mean(centred * centred, axis=-1, keepdims=True) + EPS)
    standard = centred * inverse
    standard_ref[...] = standard
    inverse_ref[...] = jnp.broadcast_to(inverse, inverse_ref.shape)
    normed = standard.astype(BF16)
    normed_ref[...] = normed
    for n in range(3):
        proj_ref[n] = dot(normed, weight_ref[n]).astype(BF16)
    proj_ref[3] = dot(delta_ref[...], weight_ref[3]).astype(BF16)

    scaling = HEAD_DIM ** (-0.5)
    low = lax.broadcasted_iota(jnp.int32, (seqs, LANES), 1) < HEAD_DIM

    def apart(pair):
        zero = jnp.zeros_like(pair)
        return jnp.concatenate([jnp.where(low, pair, zero), jnp.where(low, zero, pair)])

    def joined(rows):
        return jnp.where(low, rows[:seqs], rows[seqs:])

    def column(j, carry):
        here = pl.ds(pl.multiple_of(j * seqs, seqs), seqs)
        for pair in range(width // LANES):
            lanes = slice(pair * LANES, (pair + 1) * LANES)
            query, key, value, delta = (proj_ref[n, here, lanes] for n in range(4))
            keys, vals = apart(key), apart(value)
            scores = dot(query, keys, ((1,), (1,))) * scaling
            dprobs = dot(delta, vals, ((1,), (1,)))
            soft, dscores = [], []
            for h in range(2):
                part = scores[:, h * seqs : (h + 1) * seqs]
                exponent = jnp.exp(part - jnp.max(part, axis=-1, keepdims=True))
                prob = exponent / jnp.sum(exponent, axis=-1, keepdims=True)
                dprob = dprobs[:, h * seqs : (h + 1) * seqs]
                row_delta = jnp.sum(prob * dprob, axis=-1, keepdims=True)
                soft.append(prob.astype(BF16))
                dscores.append((prob * (dprob - row_delta)).astype(BF16))
            soft = jnp.concatenate(soft, axis=1)
            dscores = jnp.concatenate(dscores, axis=1)
            attn_ref[here, lanes] = dot(soft, vals).astype(BF16)
            grads_ref[0, here, lanes] = (dot(dscores, keys) * scaling).astype(BF16)
            key_grad = joined(dot(dscores, query, ((0,), (0,))))
            grads_ref[1, here, lanes] = (key_grad * scaling).astype(BF16)
            grads_ref[2, here, lanes] = joined(dot(soft, delta, ((0,), (0,)))).astype(BF16)
        return carry

    lax.fori_loop(0, COLS, column, 0)

    replica = replica_ref[0]
    for n in range(4):
        if n < 3:
            term = dot(normed_ref[...], grads_ref[n], ((0,), (0,)))
        else:
            term = dot(delta_ref[...], attn_ref[...], ((0,), (0,)))

        @pl.when(replica == n // 2)
        def _():
            keep_ref[n % 2] = term

        @pl.when(replica != n // 2)
        def _():
            give_ref[n % 2] = term.astype(BF16)


def input_kernel(grads_ref, delta_ref, standard_ref, inverse_ref, weight_ref, back_ref):
    groups = back_ref.shape[0] // GROUP
    tokens, width = delta_ref.shape
    seqs = tokens // COLS
    span = GROUP * ROWS
    grad_in = dot(grads_ref[0], weight_ref[0], ((1,), (1,)))
    grad_in += dot(grads_ref[1], weight_ref[1], ((1,), (1,)))
    grad_in += dot(grads_ref[2], weight_ref[2], ((1,), (1,)))
    standard = standard_ref[...]
    grad_mean = jnp.mean(grad_in, axis=-1, keepdims=True)
    grad_proj = jnp.mean(grad_in * standard, axis=-1, keepdims=True)
    branch = inverse_ref[:, :1] * (grad_in - grad_mean - standard * grad_proj)
    branch = branch.astype(BF16).astype(F32)
    input_grad = (delta_ref[...].astype(F32) + branch).astype(BF16)
    order = selection(BLOCK, lambda o: (o & 3) * 64 + (o >> 4) * 4 + ((o >> 2) & 3))
    for g in range(groups):
        rows = jnp.concatenate(
            [input_grad[j * seqs + g * span : j * seqs + (g + 1) * span] for j in range(COLS)]
        )
        back_ref[g * GROUP : (g + 1) * GROUP] = reorder(order, rows).reshape(GROUP, CELL, width)


def spread_kernel(keep_ref, got_ref, out_ref):
    quarters, held, width = out_ref.shape
    peers = held // (2 * (width // 128))
    part = width // peers
    piece = part // quarters
    block = 8 * part
    cell = 2 * piece

    def source_of(o):
        quarter = o // (8 * cell)
        rest = o - quarter * (8 * cell)
        device = rest // cell
        inside = rest - device * cell
        return (inside & 1) * block + device * part + quarter * piece + (inside >> 1)

    order = selection(2 * block, source_of)
    for g in range(peers // 8):
        here = slice(g * block, (g + 1) * block)
        rows = [(keep_ref[m, here] + got_ref[m, here].astype(F32)).astype(BF16) for m in range(2)]
        moved = reorder(order, jnp.concatenate(rows))
        for q in range(quarters):
            to = slice(g * 8 * cell, (g + 1) * 8 * cell)
            out_ref[q, to] = moved[q * 8 * cell : (q + 1) * 8 * cell]


def leave_kernel(parts_ref, back_ref, out_ref):
    peers, _, width = back_ref.shape
    out_ref[:, :CELL] = back_ref[...]
    total = jnp.sum(parts_ref[...].astype(F32), axis=0).astype(BF16)
    cell = total.shape[0] // peers
    out = lax.broadcasted_iota(jnp.int32, (peers * PAD, peers * cell), 0)
    source = lax.broadcasted_iota(jnp.int32, (peers * PAD, peers * cell), 1)
    fits = jnp.logical_and((out >> 3) * cell + (out & 7) == source, (out & 7) < cell)
    order = jnp.where(fits, 1.0, 0.0).astype(BF16)
    out_ref[:, CELL:] = reorder(order, total).reshape(peers, PAD, width)


def final_kernel(in_ref, received_ref, grads_ref):
    peers, _, width = in_ref.shape
    groups = peers // GROUP
    residues = peers * COLS
    span = GROUP * COLS
    order = selection(BLOCK, lambda o: ((o >> 2) & 15) * 16 + (o >> 6) * 4 + (o & 3))
    for g in range(groups):
        rows = in_ref[g * GROUP : (g + 1) * GROUP, :CELL].reshape(BLOCK, width)
        moved = reorder(order, rows)
        for i in range(ROWS):
            to = slice(i * residues + g * span, i * residues + (g + 1) * span)
            received_ref[to] = moved[i * span : (i + 1) * span]
    parts = in_ref[:, CELL:].astype(F32)
    quarters = NX
    parts = jnp.sum(parts.reshape(quarters, peers // quarters, PAD, width), axis=1)
    piece = grads_ref.shape[0] // quarters
    for q in range(quarters):
        for u in range(piece):
            grads_ref[q * piece + u] = parts[q, 2 * u : 2 * u + 2]


def shape(dims, dtype=BF16):
    return jax.ShapeDtypeStruct(dims, dtype)


def call(kernel, in_specs, out_shape, scratch=(), cost=(1e8, 1e6)):
    return pl.pallas_call(
        kernel,
        in_specs=in_specs,
        out_specs=jax.tree.map(lambda _: VMEM, out_shape),
        out_shape=out_shape,
        scratch_shapes=scratch,
        compiler_params=pltpu.CompilerParams(vmem_limit_bytes=14 * 1024 * 1024),
        cost_estimate=pl.CostEstimate(
            flops=int(cost[0]), bytes_accessed=int(cost[1]), transcendentals=0
        ),
    )


def exchange(array, groups=None):
    return lax.all_to_all(
        array, "mp", split_axis=0, concat_axis=0, axis_index_groups=groups, tiled=True
    )


def per_device(activations, out_grads, layer_weights):
    rows, residues, width = activations.shape[2:]
    peers = lax.axis_size("mp")
    tokens = rows * residues
    part = width // peers
    packed = call(pack_kernel, [VMEM] * 2, shape((peers, 2 * CELL, width)))(
        activations.reshape(tokens, width), out_grads.reshape(tokens, width)
    )
    arrived = exchange(packed)
    weights = layer_weights[0]
    replica = lax.axis_index("dp").astype(jnp.int32).reshape(1)
    grads, delta, standard, inverse, keep, give = call(
        attend_kernel,
        [SMEM] + [VMEM] * 2,
        (
            shape((3, tokens, width)),
            shape((tokens, width)),
            shape((tokens, width), F32),
            shape((tokens, LANES), F32),
            shape((2, width, width), F32),
            shape((2, width, width)),
        ),
        [
            pltpu.VMEM((tokens, width), BF16),
            pltpu.VMEM((tokens, width), BF16),
            pltpu.VMEM((4, tokens, width), BF16),
        ],
        cost=(3e9, 9e6),
    )(replica, arrived, weights)
    got = lax.ppermute(give, "dp", [(0, 1), (1, 0)])
    back = call(input_kernel, [VMEM] * 5, shape((peers, CELL, width)), cost=(1e9, 3e6))(
        grads, delta, standard, inverse, weights
    )
    keep, back = lax.optimization_barrier((keep, back))
    sections = lax.axis_size("section")
    back = lax.ppermute(back, "section", [(i + 1, i) for i in range(sections - 1)])
    spread = call(
        spread_kernel, [VMEM] * 2, shape((NX, 2 * width // NX, width)), cost=(1e9, 3e6)
    )(keep, got)
    ny = peers // NX
    groups = [[x * ny + y for x in range(NX)] for y in range(ny)]
    parts = exchange(spread, groups)
    leaving = call(leave_kernel, [VMEM] * 2, shape((peers, CELL + PAD, width)))(parts, back)
    landed = exchange(leaving)
    received, weight_grads = call(
        final_kernel, [VMEM], (shape((tokens, width)), shape((part, 2, width), F32))
    )(landed)
    return (received.reshape(activations.shape), weight_grads.transpose(1, 0, 2)[None])


def solution(mesh):
    in_specs = (
        P("dp", "section", "mp", None, None),
        P("dp", "section", "mp", None, None),
        P("section", None, None, None),
    )
    out_specs = (P("dp", "section", "mp", None, None), P("section", "dp", "mp", None))

    return jax.shard_map(
        per_device, mesh=mesh, in_specs=in_specs, out_specs=out_specs, check_vma=False
    )
```

```python
import jax
import jax.numpy as jnp
from jax import lax
from jax.experimental import pallas as pl
from jax.experimental.pallas import tpu as pltpu
from jax.sharding import PartitionSpec as P


HEAD_DIM = 64
EPS = 1e-05
F32 = jnp.float32
BF16 = jnp.bfloat16
LANES = 128
ROWS = 4
COLS = 4
CELL = ROWS * COLS
GROUP = 16
BLOCK = GROUP * CELL
NX = 4
PAD = 8
VMEM = pl.BlockSpec(memory_space=pltpu.VMEM)
HBM = pl.BlockSpec(memory_space=pltpu.HBM)
SMEM = pl.BlockSpec(memory_space=pltpu.SMEM)


def dot(a, b, dims=((1,), (0,))):
    return lax.dot_general(a, b, (dims, ((), ())), preferred_element_type=F32)


def selection(size, source_of):
    out = lax.broadcasted_iota(jnp.int32, (size, size), 0)
    source = lax.broadcasted_iota(jnp.int32, (size, size), 1)
    return jnp.where(source_of(out) == source, 1.0, 0.0).astype(BF16)


def reorder(matrix, rows):
    return dot(matrix, rows).astype(BF16)


def pack_kernel(act_ref, grad_ref, out_ref, held_ref, sems):
    copies = [
        pltpu.make_async_copy(ref, held_ref.at[slot], sems.at[slot])
        for slot, ref in enumerate((act_ref, grad_ref))
    ]
    for copy in copies:
        copy.start()
    order = selection(BLOCK, lambda o: ((o >> 2) & 3) * 64 + (o >> 4) * 4 + (o & 3))
    groups = out_ref.shape[0] // GROUP
    residues = act_ref.shape[0] // ROWS
    span = GROUP * COLS
    for slot, copy in enumerate(copies):
        copy.wait()
        for g in range(groups):
            starts = [i * residues + g * span for i in range(ROWS)]
            rows = jnp.concatenate([held_ref[slot, at : at + span] for at in starts])
            moved = reorder(order, rows).reshape(GROUP, CELL, -1)
            out_ref[g * GROUP : (g + 1) * GROUP, slot * CELL : (slot + 1) * CELL] = moved


def attend_kernel(
    replica_ref,
    in_ref,
    weight_ref,
    grads_ref,
    delta_ref,
    standard_ref,
    inverse_ref,
    keep_ref,
    give_ref,
    normed_ref,
    attn_ref,
    proj_ref,
):
    peers = in_ref.shape[0]
    groups = peers // GROUP
    width = in_ref.shape[2]
    seqs = peers * ROWS
    span = GROUP * ROWS
    order = selection(BLOCK, lambda o: ((o >> 2) & 15) * 16 + (o & 3) * 4 + (o >> 6))
    for g in range(groups):
        peers_of = slice(g * GROUP, (g + 1) * GROUP)
        acts = dot(order, in_ref[peers_of, :CELL].reshape(BLOCK, width))
        outs = reorder(order, in_ref[peers_of, CELL : 2 * CELL].reshape(BLOCK, width))
        for j in range(COLS):
            to = slice(j * seqs + g * span, j * seqs + (g + 1) * span)
            standard_ref[to] = acts[j * span : (j + 1) * span]
            delta_ref[to] = outs[j * span : (j + 1) * span]
    values = standard_ref[...]
    mean_value = jnp.mean(values, axis=-1, keepdims=True)
    centred = values - mean_value
    inverse = lax.rsqrt(jnp.mean(centred * centred, axis=-1, keepdims=True) + EPS)
    standard = centred * inverse
    standard_ref[...] = standard
    inverse_ref[...] = jnp.broadcast_to(inverse, inverse_ref.shape)
    normed = standard.astype(BF16)
    normed_ref[...] = normed
    joint = jnp.concatenate([weight_ref[n] for n in range(3)], axis=1)
    proj_ref[:, : 3 * width] = dot(normed, joint).astype(BF16)
    proj_ref[:, 3 * width :] = dot(delta_ref[...], weight_ref[3]).astype(BF16)

    scaling = HEAD_DIM ** (-0.5)
    low = lax.broadcasted_iota(jnp.int32, (seqs, LANES), 1) < HEAD_DIM

    def apart(pair):
        zero = jnp.zeros_like(pair)
        return jnp.concatenate([jnp.where(low, pair, zero), jnp.where(low, zero, pair)])

    def joined(rows):
        return jnp.where(low, rows[:seqs], rows[seqs:])

    def column(j, carry):
        here = pl.ds(pl.multiple_of(j * seqs, seqs), seqs)
        pairs = range(width // LANES)
        loaded = [
            [proj_ref[here, n * width + p * LANES : n * width + (p + 1) * LANES] for n in range(4)]
            for p in pairs
        ]
        split = [(apart(key), apart(value)) for _, key, value, _ in loaded]
        scores = [dot(split[p][0], loaded[p][0], ((1,), (1,))) * scaling for p in pairs]
        dprobs = [dot(split[p][1], loaded[p][3], ((1,), (1,))) for p in pairs]
        for p in pairs:
            query, _, _, delta = loaded[p]
            keys, vals = split[p]
            soft, dscores = [], []
            for h in range(2):
                part = scores[p][h * seqs : (h + 1) * seqs]
                exponent = jnp.exp(part - jnp.max(part, axis=0, keepdims=True))
                prob = exponent * (1.0 / jnp.sum(exponent, axis=0, keepdims=True))
                dprob = dprobs[p][h * seqs : (h + 1) * seqs]
                column_delta = jnp.sum(prob * dprob, axis=0, keepdims=True)
                soft.append(prob.astype(BF16))
                dscores.append((prob * (dprob - column_delta)).astype(BF16))
            soft = jnp.concatenate(soft)
            dscores = jnp.concatenate(dscores)
            lanes = [slice(n * width + p * LANES, n * width + (p + 1) * LANES) for n in range(3)]
            attn_ref[here, lanes[0]] = dot(soft, vals, ((0,), (0,))).astype(BF16)
            query_grad = dot(dscores, keys, ((0,), (0,)))
            grads_ref[here, lanes[0]] = (query_grad * scaling).astype(BF16)
            grads_ref[here, lanes[1]] = (joined(dot(dscores, query)) * scaling).astype(BF16)
            grads_ref[here, lanes[2]] = joined(dot(soft, delta)).astype(BF16)
        return carry

    lax.fori_loop(0, COLS, column, 0)

    first = replica_ref[0] == 0
    term = dot(normed_ref[...], grads_ref[...], ((0,), (0,)))
    terms = [term[:, n * width : (n + 1) * width] for n in range(3)]
    terms.append(dot(delta_ref[...], attn_ref[...], ((0,), (0,))))
    for m in range(2):
        keep_ref[m] = jnp.where(first, terms[m], terms[m + 2])
        give_ref[m] = jnp.where(first, terms[m + 2], terms[m]).astype(BF16)


def input_kernel(grads_ref, delta_ref, standard_ref, inverse_ref, weight_ref, back_ref):
    groups = back_ref.shape[0] // GROUP
    tokens, width = delta_ref.shape
    seqs = tokens // COLS
    span = GROUP * ROWS
    joint = jnp.concatenate([weight_ref[n] for n in range(3)], axis=1)
    grad_in = dot(grads_ref[...], joint, ((1,), (1,)))
    standard = standard_ref[...]
    grad_mean = jnp.mean(grad_in, axis=-1, keepdims=True)
    grad_proj = jnp.mean(grad_in * standard, axis=-1, keepdims=True)
    branch = inverse_ref[:, :1] * (grad_in - grad_mean - standard * grad_proj)
    branch = branch.astype(BF16).astype(F32)
    input_grad = (delta_ref[...].astype(F32) + branch).astype(BF16)
    order = selection(BLOCK, lambda o: (o & 3) * 64 + (o >> 4) * 4 + ((o >> 2) & 3))
    for g in range(groups):
        rows = jnp.concatenate(
            [input_grad[j * seqs + g * span : j * seqs + (g + 1) * span] for j in range(COLS)]
        )
        back_ref[g * GROUP : (g + 1) * GROUP] = reorder(order, rows).reshape(GROUP, CELL, width)


def spread_kernel(keep_ref, got_ref, out_ref):
    quarters, held, width = out_ref.shape
    peers = held // (2 * (width // 128))
    part = width // peers
    piece = part // quarters
    block = 8 * part
    cell = 2 * piece

    def source_of(o):
        quarter = o // (8 * cell)
        rest = o - quarter * (8 * cell)
        device = rest // cell
        inside = rest - device * cell
        return (inside & 1) * block + device * part + quarter * piece + (inside >> 1)

    order = selection(2 * block, source_of)
    for g in range(peers // 8):
        here = slice(g * block, (g + 1) * block)
        rows = [(keep_ref[m, here] + got_ref[m, here].astype(F32)).astype(BF16) for m in range(2)]
        moved = reorder(order, jnp.concatenate(rows))
        for q in range(quarters):
            to = slice(g * 8 * cell, (g + 1) * 8 * cell)
            out_ref[q, to] = moved[q * 8 * cell : (q + 1) * 8 * cell]


def leave_kernel(parts_ref, back_ref, out_ref):
    peers, _, width = back_ref.shape
    out_ref[:, :CELL] = back_ref[...]
    total = jnp.sum(parts_ref[...].astype(F32), axis=0).astype(BF16)
    cell = total.shape[0] // peers
    out = lax.broadcasted_iota(jnp.int32, (peers * PAD, peers * cell), 0)
    source = lax.broadcasted_iota(jnp.int32, (peers * PAD, peers * cell), 1)
    fits = jnp.logical_and((out >> 3) * cell + (out & 7) == source, (out & 7) < cell)
    order = jnp.where(fits, 1.0, 0.0).astype(BF16)
    out_ref[:, CELL:] = reorder(order, total).reshape(peers, PAD, width)


def final_kernel(in_ref, received_ref, grads_ref):
    peers, _, width = in_ref.shape
    groups = peers // GROUP
    residues = peers * COLS
    span = GROUP * COLS
    order = selection(BLOCK, lambda o: ((o >> 2) & 15) * 16 + (o >> 6) * 4 + (o & 3))
    for g in range(groups):
        rows = in_ref[g * GROUP : (g + 1) * GROUP, :CELL].reshape(BLOCK, width)
        moved = reorder(order, rows)
        for i in range(ROWS):
            to = slice(i * residues + g * span, i * residues + (g + 1) * span)
            received_ref[to] = moved[i * span : (i + 1) * span]
    parts = in_ref[:, CELL:].astype(F32)
    quarters = NX
    parts = jnp.sum(parts.reshape(quarters, peers // quarters, PAD, width), axis=1)
    piece = grads_ref.shape[0] // quarters
    for q in range(quarters):
        for u in range(piece):
            grads_ref[q * piece + u] = parts[q, 2 * u : 2 * u + 2]


def shape(dims, dtype=BF16):
    return jax.ShapeDtypeStruct(dims, dtype)


def call(kernel, in_specs, out_shape, scratch=(), cost=(1e8, 1e6), mib=14):
    return pl.pallas_call(
        kernel,
        in_specs=in_specs,
        out_specs=jax.tree.map(lambda _: VMEM, out_shape),
        out_shape=out_shape,
        scratch_shapes=scratch,
        compiler_params=pltpu.CompilerParams(vmem_limit_bytes=mib * 1024 * 1024),
        cost_estimate=pl.CostEstimate(
            flops=int(cost[0]), bytes_accessed=int(cost[1]), transcendentals=0
        ),
    )


def exchange(array, groups=None):
    return lax.all_to_all(
        array, "mp", split_axis=0, concat_axis=0, axis_index_groups=groups, tiled=True
    )


def per_device(activations, out_grads, layer_weights):
    rows, residues, width = activations.shape[2:]
    peers = lax.axis_size("mp")
    tokens = rows * residues
    part = width // peers
    packed = call(
        pack_kernel,
        [HBM] * 2,
        shape((peers, 2 * CELL, width)),
        [pltpu.VMEM((2, tokens, width), BF16), pltpu.SemaphoreType.DMA((2,))],
        mib=56,
    )(
        activations.reshape(tokens, width), out_grads.reshape(tokens, width)
    )
    arrived = exchange(packed)
    weights = layer_weights[0]
    replica = lax.axis_index("dp").astype(jnp.int32).reshape(1)
    grads, delta, standard, inverse, keep, give = call(
        attend_kernel,
        [SMEM] + [VMEM] * 2,
        (
            shape((tokens, 3 * width)),
            shape((tokens, width)),
            shape((tokens, width), F32),
            shape((tokens, LANES), F32),
            shape((2, width, width), F32),
            shape((2, width, width)),
        ),
        [
            pltpu.VMEM((tokens, width), BF16),
            pltpu.VMEM((tokens, width), BF16),
            pltpu.VMEM((tokens, 4 * width), BF16),
        ],
        cost=(3e9, 9e6),
    )(replica, arrived, weights)
    got = lax.ppermute(give, "dp", [(0, 1), (1, 0)])
    back = call(input_kernel, [VMEM] * 5, shape((peers, CELL, width)), cost=(1e9, 3e6))(
        grads, delta, standard, inverse, weights
    )
    keep, back = lax.optimization_barrier((keep, back))
    sections = lax.axis_size("section")
    back = lax.ppermute(back, "section", [(i + 1, i) for i in range(sections - 1)])
    spread = call(
        spread_kernel, [VMEM] * 2, shape((NX, 2 * width // NX, width)), cost=(1e9, 3e6)
    )(keep, got)
    ny = peers // NX
    groups = [[x * ny + y for x in range(NX)] for y in range(ny)]
    parts = exchange(spread, groups)
    leaving = call(leave_kernel, [VMEM] * 2, shape((peers, CELL + PAD, width)))(parts, back)
    landed = exchange(leaving)
    received, weight_grads = call(
        final_kernel, [VMEM], (shape((tokens, width)), shape((part, 2, width), F32))
    )(landed)
    return (received.reshape(activations.shape), weight_grads.transpose(1, 0, 2)[None])


def solution(mesh):
    in_specs = (
        P("dp", "section", "mp", None, None),
        P("dp", "section", "mp", None, None),
        P("section", None, None, None),
    )
    out_specs = (P("dp", "section", "mp", None, None), P("section", "dp", "mp", None))

    return jax.shard_map(
        per_device, mesh=mesh, in_specs=in_specs, out_specs=out_specs, check_vma=False
    )
```

```python
import jax
import jax.numpy as jnp
from jax import lax
from jax.experimental import pallas as pl
from jax.experimental.pallas import tpu as pltpu
from jax.sharding import PartitionSpec as P


HEAD_DIM = 64
EPS = 1e-05
F32 = jnp.float32
BF16 = jnp.bfloat16
LANES = 128
ROWS = 4
COLS = 4
CELL = ROWS * COLS
GROUP = 16
BLOCK = GROUP * CELL
NX = 4
NY = 8
VMEM = pl.BlockSpec(memory_space=pltpu.VMEM)
HBM = pl.BlockSpec(memory_space=pltpu.HBM)
SMEM = pl.BlockSpec(memory_space=pltpu.SMEM)


def dot(a, b, dims=((1,), (0,))):
    return lax.dot_general(a, b, (dims, ((), ())), preferred_element_type=F32)


def selection(size, source_of):
    out = lax.broadcasted_iota(jnp.int32, (size, size), 0)
    source = lax.broadcasted_iota(jnp.int32, (size, size), 1)
    return jnp.where(source_of(out) == source, 1.0, 0.0).astype(BF16)


def reorder(matrix, rows):
    return dot(matrix, rows).astype(BF16)


def pack_kernel(act_ref, grad_ref, out_ref, held_ref, sems):
    copies = [
        pltpu.make_async_copy(ref, held_ref.at[slot], sems.at[slot])
        for slot, ref in enumerate((act_ref, grad_ref))
    ]
    for copy in copies:
        copy.start()
    order = selection(BLOCK, lambda o: ((o >> 2) & 3) * 64 + (o >> 4) * 4 + (o & 3))
    groups = out_ref.shape[0] // GROUP
    residues = act_ref.shape[0] // ROWS
    span = GROUP * COLS
    for slot, copy in enumerate(copies):
        copy.wait()
        for g in range(groups):
            starts = [i * residues + g * span for i in range(ROWS)]
            rows = jnp.concatenate([held_ref[slot, at : at + span] for at in starts])
            moved = reorder(order, rows).reshape(GROUP, CELL, -1)
            out_ref[g * GROUP : (g + 1) * GROUP, slot * CELL : (slot + 1) * CELL] = moved


def attend_kernel(
    replica_ref,
    in_ref,
    weight_ref,
    grads_ref,
    delta_ref,
    standard_ref,
    inverse_ref,
    keep_ref,
    give_ref,
    normed_ref,
    attn_ref,
    proj_ref,
):
    peers = in_ref.shape[0]
    groups = peers // GROUP
    width = in_ref.shape[2]
    seqs = peers * ROWS
    span = GROUP * ROWS
    order = selection(BLOCK, lambda o: ((o >> 2) & 15) * 16 + (o & 3) * 4 + (o >> 6))
    for g in range(groups):
        peers_of = slice(g * GROUP, (g + 1) * GROUP)
        acts = dot(order, in_ref[peers_of, :CELL].reshape(BLOCK, width))
        outs = reorder(order, in_ref[peers_of, CELL : 2 * CELL].reshape(BLOCK, width))
        for j in range(COLS):
            to = slice(j * seqs + g * span, j * seqs + (g + 1) * span)
            standard_ref[to] = acts[j * span : (j + 1) * span]
            delta_ref[to] = outs[j * span : (j + 1) * span]
    values = standard_ref[...]
    mean_value = jnp.mean(values, axis=-1, keepdims=True)
    centred = values - mean_value
    inverse = lax.rsqrt(jnp.mean(centred * centred, axis=-1, keepdims=True) + EPS)
    standard = centred * inverse
    standard_ref[...] = standard
    inverse_ref[...] = jnp.broadcast_to(inverse, inverse_ref.shape)
    normed = standard.astype(BF16)
    normed_ref[...] = normed
    joint = jnp.concatenate([weight_ref[n] for n in range(3)], axis=1)
    proj_ref[:, : 3 * width] = dot(normed, joint).astype(BF16)
    proj_ref[:, 3 * width :] = dot(delta_ref[...], weight_ref[3]).astype(BF16)

    scaling = HEAD_DIM ** (-0.5)
    low = lax.broadcasted_iota(jnp.int32, (seqs, LANES), 1) < HEAD_DIM

    def apart(pair):
        zero = jnp.zeros_like(pair)
        return jnp.concatenate([jnp.where(low, pair, zero), jnp.where(low, zero, pair)])

    def joined(rows):
        return jnp.where(low, rows[:seqs], rows[seqs:])

    def column(j, carry):
        here = pl.ds(pl.multiple_of(j * seqs, seqs), seqs)
        pairs = range(width // LANES)
        loaded = [
            [proj_ref[here, n * width + p * LANES : n * width + (p + 1) * LANES] for n in range(4)]
            for p in pairs
        ]
        split = [(apart(key), apart(value)) for _, key, value, _ in loaded]
        scores = [dot(split[p][0], loaded[p][0], ((1,), (1,))) * scaling for p in pairs]
        dprobs = [dot(split[p][1], loaded[p][3], ((1,), (1,))) for p in pairs]
        for p in pairs:
            query, _, _, delta = loaded[p]
            keys, vals = split[p]
            soft, dscores = [], []
            for h in range(2):
                part = scores[p][h * seqs : (h + 1) * seqs]
                exponent = jnp.exp(part - jnp.max(part, axis=0, keepdims=True))
                prob = exponent * (1.0 / jnp.sum(exponent, axis=0, keepdims=True))
                dprob = dprobs[p][h * seqs : (h + 1) * seqs]
                column_delta = jnp.sum(prob * dprob, axis=0, keepdims=True)
                soft.append(prob.astype(BF16))
                dscores.append((prob * (dprob - column_delta)).astype(BF16))
            soft = jnp.concatenate(soft)
            dscores = jnp.concatenate(dscores)
            lanes = [slice(n * width + p * LANES, n * width + (p + 1) * LANES) for n in range(3)]
            attn_ref[here, lanes[0]] = dot(soft, vals, ((0,), (0,))).astype(BF16)
            query_grad = dot(dscores, keys, ((0,), (0,)))
            grads_ref[here, lanes[0]] = (query_grad * scaling).astype(BF16)
            grads_ref[here, lanes[1]] = (joined(dot(dscores, query)) * scaling).astype(BF16)
            grads_ref[here, lanes[2]] = joined(dot(soft, delta)).astype(BF16)
        return carry

    lax.fori_loop(0, COLS, column, 0)

    first = replica_ref[0] == 0
    term = dot(normed_ref[...], grads_ref[...], ((0,), (0,)))
    terms = [term[:, n * width : (n + 1) * width] for n in range(3)]
    terms.append(dot(delta_ref[...], attn_ref[...], ((0,), (0,))))
    for m in range(2):
        keep_ref[m] = jnp.where(first, terms[m], terms[m + 2])
        give_ref[m] = jnp.where(first, terms[m + 2], terms[m]).astype(BF16)


def input_kernel(grads_ref, delta_ref, standard_ref, inverse_ref, weight_ref, back_ref):
    groups = back_ref.shape[0] // GROUP
    tokens, width = delta_ref.shape
    seqs = tokens // COLS
    span = GROUP * ROWS
    joint = jnp.concatenate([weight_ref[n] for n in range(3)], axis=1)
    grad_in = dot(grads_ref[...], joint, ((1,), (1,)))
    standard = standard_ref[...]
    grad_mean = jnp.mean(grad_in, axis=-1, keepdims=True)
    grad_proj = jnp.mean(grad_in * standard, axis=-1, keepdims=True)
    branch = inverse_ref[:, :1] * (grad_in - grad_mean - standard * grad_proj)
    branch = branch.astype(BF16).astype(F32)
    input_grad = (delta_ref[...].astype(F32) + branch).astype(BF16)
    order = selection(BLOCK, lambda o: (o & 3) * 64 + (o >> 4) * 4 + ((o >> 2) & 3))
    for g in range(groups):
        rows = jnp.concatenate(
            [input_grad[j * seqs + g * span : j * seqs + (g + 1) * span] for j in range(COLS)]
        )
        back_ref[g * GROUP : (g + 1) * GROUP] = reorder(order, rows).reshape(GROUP, CELL, width)


def spread_kernel(place_ref, keep_ref, got_ref, hold_ref, send_ref):
    part = hold_ref.shape[2]
    x = lax.div(place_ref[0], NY)
    near = x + 1 - 2 * lax.rem(x, 2)
    for ref, blocks in ((hold_ref, (x, NX - 1 - x)), (send_ref, (near, NX - 1 - near))):
        for slot, block in enumerate(blocks):
            rows = pl.ds(pl.multiple_of(block * part, part), part)
            for m in range(2):
                total = keep_ref[m, rows] + got_ref[m, rows].astype(F32)
                ref[slot, m] = total.astype(ref.dtype)


def halve_kernel(hold_ref, got_ref, own_ref, send_ref):
    own_ref[...] = hold_ref[0] + got_ref[0].astype(F32)
    send_ref[...] = (hold_ref[1] + got_ref[1].astype(F32)).astype(BF16)


def order_kernel(own_ref, got_ref, out_ref):
    peers, held, width = out_ref.shape
    part = held // 2
    size = peers * held

    def source_of(o):
        peer = o // held
        inside = o - peer * held
        return (inside & 1) * (size // 2) + peer * part + (inside >> 1)

    rows = (own_ref[...] + got_ref[...].astype(F32)).astype(BF16).reshape(size, width)
    out_ref[...] = reorder(selection(size, source_of), rows).reshape(peers, held, width)


def total_kernel(in_ref, out_ref):
    total = jnp.sum(in_ref[...].astype(F32), axis=0)
    for row in range(out_ref.shape[0]):
        out_ref[row] = total[2 * row : 2 * row + 2]


def unpack_kernel(in_ref, out_ref):
    peers, _, width = in_ref.shape
    residues = peers * COLS
    span = GROUP * COLS
    order = selection(BLOCK, lambda o: ((o >> 2) & 15) * 16 + (o >> 6) * 4 + (o & 3))
    for g in range(peers // GROUP):
        rows = in_ref[g * GROUP : (g + 1) * GROUP].reshape(BLOCK, width)
        moved = reorder(order, rows)
        for i in range(ROWS):
            to = slice(i * residues + g * span, i * residues + (g + 1) * span)
            out_ref[to] = moved[i * span : (i + 1) * span]


def shape(dims, dtype=BF16):
    return jax.ShapeDtypeStruct(dims, dtype)


def call(kernel, in_specs, out_shape, scratch=(), cost=(1e8, 1e6), mib=14):
    return pl.pallas_call(
        kernel,
        in_specs=in_specs,
        out_specs=jax.tree.map(lambda _: VMEM, out_shape),
        out_shape=out_shape,
        scratch_shapes=scratch,
        compiler_params=pltpu.CompilerParams(vmem_limit_bytes=mib * 1024 * 1024),
        cost_estimate=pl.CostEstimate(
            flops=int(cost[0]), bytes_accessed=int(cost[1]), transcendentals=0
        ),
    )


def exchange(array, groups=None):
    return lax.all_to_all(
        array, "mp", split_axis=0, concat_axis=0, axis_index_groups=groups, tiled=True
    )


def per_device(activations, out_grads, layer_weights):
    rows, residues, width = activations.shape[2:]
    peers = lax.axis_size("mp")
    tokens = rows * residues
    part = width // peers
    packed = call(
        pack_kernel,
        [HBM] * 2,
        shape((peers, 2 * CELL, width)),
        [pltpu.VMEM((2, tokens, width), BF16), pltpu.SemaphoreType.DMA((2,))],
        mib=56,
    )(
        activations.reshape(tokens, width), out_grads.reshape(tokens, width)
    )
    arrived = exchange(packed)
    weights = layer_weights[0]
    replica = lax.axis_index("dp").astype(jnp.int32).reshape(1)
    grads, delta, standard, inverse, keep, give = call(
        attend_kernel,
        [SMEM] + [VMEM] * 2,
        (
            shape((tokens, 3 * width)),
            shape((tokens, width)),
            shape((tokens, width), F32),
            shape((tokens, LANES), F32),
            shape((2, width, width), F32),
            shape((2, width, width)),
        ),
        [
            pltpu.VMEM((tokens, width), BF16),
            pltpu.VMEM((tokens, width), BF16),
            pltpu.VMEM((tokens, 4 * width), BF16),
        ],
        cost=(3e9, 9e6),
    )(replica, arrived, weights)
    got = lax.ppermute(give, "dp", [(0, 1), (1, 0)])
    back = call(input_kernel, [VMEM] * 5, shape((peers, CELL, width)), cost=(1e9, 3e6))(
        grads, delta, standard, inverse, weights
    )
    landed = exchange(back)

    ny = NY
    block = width // NX
    place = lax.axis_index("mp").astype(jnp.int32).reshape(1)

    def over_x(array, partner_of):
        pairs = [(q * ny + y, partner_of(q) * ny + y) for q in range(NX) for y in range(ny)]
        return lax.ppermute(array, "mp", pairs)

    hold, send = call(
        spread_kernel,
        [SMEM] + [VMEM] * 2,
        (shape((2, 2, block, width), F32), shape((2, 2, block, width))),
    )(place, keep, got)
    got = over_x(send, lambda q: q ^ 1)
    own, send = call(
        halve_kernel, [VMEM] * 2, (shape((2, block, width), F32), shape((2, block, width)))
    )(hold, got)
    got = over_x(send, lambda q: NX - 1 - q)

    sections = lax.axis_size("section")
    received = call(unpack_kernel, [VMEM], shape((tokens, width)))(landed)
    received = lax.ppermute(received, "section", [(i + 1, i) for i in range(sections - 1)])

    parts = call(order_kernel, [VMEM] * 2, shape((ny, 2 * part, width)))(own, got)
    parts = exchange(parts, [[q * ny + y for y in range(ny)] for q in range(NX)])
    weight_grads = call(total_kernel, [VMEM], shape((part, 2, width), F32))(parts)
    return (received.reshape(activations.shape), weight_grads.transpose(1, 0, 2)[None])


def solution(mesh):
    in_specs = (
        P("dp", "section", "mp", None, None),
        P("dp", "section", "mp", None, None),
        P("section", None, None, None),
    )
    out_specs = (P("dp", "section", "mp", None, None), P("section", "dp", "mp", None))

    return jax.shard_map(
        per_device, mesh=mesh, in_specs=in_specs, out_specs=out_specs, check_vma=False
    )
```

```python
import jax
import jax.numpy as jnp
from jax import lax
from jax.experimental import pallas as pl
from jax.experimental.pallas import tpu as pltpu
from jax.sharding import PartitionSpec as P


HEAD_DIM = 64
EPS = 1e-05
F32 = jnp.float32
BF16 = jnp.bfloat16
LANES = 128
ROWS = 4
COLS = 4
HALF = COLS // 2
CELL = ROWS * COLS
GROUP = 16
BLOCK = GROUP * CELL
NX = 4
NY = 8
PAD = 8
VMEM = pl.BlockSpec(memory_space=pltpu.VMEM)
HBM = pl.BlockSpec(memory_space=pltpu.HBM)
SMEM = pl.BlockSpec(memory_space=pltpu.SMEM)


def dot(a, b, dims=((1,), (0,))):
    return lax.dot_general(a, b, (dims, ((), ())), preferred_element_type=F32)


def selection(size, source_of):
    out = lax.broadcasted_iota(jnp.int32, size, 0)
    source = lax.broadcasted_iota(jnp.int32, size, 1)
    return jnp.where(source_of(out) == source, 1.0, 0.0).astype(BF16)


def reorder(matrix, rows):
    return dot(matrix, rows).astype(BF16)


def pack_kernel(act_ref, grad_ref, out_ref, held_ref, sems):
    copies = [
        pltpu.make_async_copy(ref, held_ref.at[slot], sems.at[slot])
        for slot, ref in enumerate((act_ref, grad_ref))
    ]
    for copy in copies:
        copy.start()
    order = selection((BLOCK, BLOCK), lambda o: ((o >> 2) & 3) * 64 + (o >> 4) * 4 + (o & 3))
    groups = out_ref.shape[0] // GROUP
    residues = act_ref.shape[0] // ROWS
    span = GROUP * COLS
    for slot, copy in enumerate(copies):
        copy.wait()
        for g in range(groups):
            starts = [i * residues + g * span for i in range(ROWS)]
            rows = jnp.concatenate([held_ref[slot, at : at + span] for at in starts])
            moved = reorder(order, rows).reshape(GROUP, CELL, -1)
            out_ref[g * GROUP : (g + 1) * GROUP, slot * CELL : (slot + 1) * CELL] = moved


def attend(first, in_ref, weight_ref, joint, refs, scratch):
    back_ref, normed_ref, delta_ref, grads_ref, attn_ref = refs
    standard_ref, proj_ref = scratch
    peers, _, width = in_ref.shape
    groups = peers // GROUP
    seqs = peers * ROWS
    span = GROUP * ROWS

    def source_of(o):
        return ((o >> 2) & 15) * CELL + (o & 3) * COLS + (o >> 6) + first

    order = selection((HALF * span, BLOCK), source_of)
    for g in range(groups):
        peers_of = slice(g * GROUP, (g + 1) * GROUP)
        acts = dot(order, in_ref[peers_of, :CELL].reshape(BLOCK, width))
        outs = reorder(order, in_ref[peers_of, CELL : 2 * CELL].reshape(BLOCK, width))
        for j in range(HALF):
            to = slice(j * seqs + g * span, j * seqs + (g + 1) * span)
            standard_ref[to] = acts[j * span : (j + 1) * span]
            delta_ref[to] = outs[j * span : (j + 1) * span]
    values = standard_ref[...]
    mean_value = jnp.mean(values, axis=-1, keepdims=True)
    centred = values - mean_value
    inverse = lax.rsqrt(jnp.mean(centred * centred, axis=-1, keepdims=True) + EPS)
    standard = centred * inverse
    standard_ref[...] = standard
    normed = standard.astype(BF16)
    normed_ref[...] = normed
    proj_ref[:, : 3 * width] = dot(normed, joint).astype(BF16)
    proj_ref[:, 3 * width :] = dot(delta_ref[...], weight_ref[3]).astype(BF16)

    scaling = HEAD_DIM ** (-0.5)
    low = lax.broadcasted_iota(jnp.int32, (seqs, LANES), 1) < HEAD_DIM

    def apart(pair):
        zero = jnp.zeros_like(pair)
        return jnp.concatenate([jnp.where(low, pair, zero), jnp.where(low, zero, pair)])

    def joined(rows):
        return jnp.where(low, rows[:seqs], rows[seqs:])

    def column(j, carry):
        here = pl.ds(pl.multiple_of(j * seqs, seqs), seqs)
        pairs = range(width // LANES)
        loaded = [
            [proj_ref[here, n * width + p * LANES : n * width + (p + 1) * LANES] for n in range(4)]
            for p in pairs
        ]
        split = [(apart(key), apart(value)) for _, key, value, _ in loaded]
        scores = [dot(split[p][0], loaded[p][0], ((1,), (1,))) * scaling for p in pairs]
        dprobs = [dot(split[p][1], loaded[p][3], ((1,), (1,))) for p in pairs]
        for p in pairs:
            query, _, _, delta = loaded[p]
            keys, vals = split[p]
            soft, dscores = [], []
            for h in range(2):
                part = scores[p][h * seqs : (h + 1) * seqs]
                exponent = jnp.exp(part - jnp.max(part, axis=0, keepdims=True))
                prob = exponent * (1.0 / jnp.sum(exponent, axis=0, keepdims=True))
                dprob = dprobs[p][h * seqs : (h + 1) * seqs]
                column_delta = jnp.sum(prob * dprob, axis=0, keepdims=True)
                soft.append(prob.astype(BF16))
                dscores.append((prob * (dprob - column_delta)).astype(BF16))
            soft = jnp.concatenate(soft)
            dscores = jnp.concatenate(dscores)
            lanes = [slice(n * width + p * LANES, n * width + (p + 1) * LANES) for n in range(3)]
            attn_ref[here, lanes[0]] = dot(soft, vals, ((0,), (0,))).astype(BF16)
            query_grad = dot(dscores, keys, ((0,), (0,)))
            grads_ref[here, lanes[0]] = (query_grad * scaling).astype(BF16)
            grads_ref[here, lanes[1]] = (joined(dot(dscores, query)) * scaling).astype(BF16)
            grads_ref[here, lanes[2]] = joined(dot(soft, delta)).astype(BF16)
        return carry

    lax.fori_loop(0, HALF, column, 0)

    grad_in = dot(grads_ref[...], joint, ((1,), (1,)))
    standard = standard_ref[...]
    grad_mean = jnp.mean(grad_in, axis=-1, keepdims=True)
    grad_proj = jnp.mean(grad_in * standard, axis=-1, keepdims=True)
    branch = inverse * (grad_in - grad_mean - standard * grad_proj)
    branch = branch.astype(BF16).astype(F32)
    input_grad = (delta_ref[...].astype(F32) + branch).astype(BF16)

    def back_from(o):
        return (o & 1) * span + (o >> 3) * ROWS + ((o >> 1) & 3)

    order = selection((HALF * span, HALF * span), back_from)
    for g in range(groups):
        rows = jnp.concatenate(
            [input_grad[j * seqs + g * span : j * seqs + (g + 1) * span] for j in range(HALF)]
        )
        moved = reorder(order, rows).reshape(GROUP, CELL // 2, width)
        back_ref[g * GROUP : (g + 1) * GROUP] = moved


def early_kernel(in_ref, weight_ref, *refs):
    joint = jnp.concatenate([weight_ref[n] for n in range(3)], axis=1)
    attend(0, in_ref, weight_ref, joint, refs[:5], refs[5:])


def late_kernel(
    replica_ref,
    in_ref,
    weight_ref,
    early_normed_ref,
    early_delta_ref,
    early_grads_ref,
    early_attn_ref,
    back_ref,
    keep_ref,
    give_ref,
    normed_ref,
    delta_ref,
    grads_ref,
    attn_ref,
    standard_ref,
    proj_ref,
    terms_ref,
):
    joint = jnp.concatenate([weight_ref[n] for n in range(3)], axis=1)
    refs = (back_ref, normed_ref, delta_ref, grads_ref, attn_ref)
    attend(HALF, in_ref, weight_ref, joint, refs, (standard_ref, proj_ref))
    width = in_ref.shape[2]
    down = ((0,), (0,))
    first = replica_ref[0] == 0
    term = dot(early_normed_ref[...], early_grads_ref[...], down)
    term += dot(normed_ref[...], grads_ref[...], down)
    terms = [term[:, n * width : (n + 1) * width] for n in range(3)]
    term = dot(early_delta_ref[...], early_attn_ref[...], down)
    terms.append(term + dot(delta_ref[...], attn_ref[...], down))
    tiles = [slice(n * LANES, (n + 1) * LANES) for n in range(width // LANES)]
    for m in range(2):
        kept = jnp.where(first, terms[m], terms[m + 2])
        given = jnp.where(first, terms[m + 2], terms[m])
        for n, lanes in enumerate(tiles):
            terms_ref[m, n] = kept[:, lanes]
            terms_ref[2 + m, n] = given[:, lanes]
    peers = in_ref.shape[0]
    part = width // peers
    piece = part // NX
    for q in range(NX):
        for u in range(piece):
            for m in range(2):
                to = slice((2 * u + m) * peers, (2 * u + m + 1) * peers)
                rows = pl.ds(q * piece + u, peers, stride=part)
                for n, lanes in enumerate(tiles):
                    keep_ref[q, to, lanes] = terms_ref[m, n, rows]
                    give_ref[q, to, lanes] = terms_ref[2 + m, n, rows].astype(BF16)


def beside(x):
    return x + 1 - 2 * lax.rem(x, 2)


def across(x):
    return NX - 1 - x


def spread_kernel(place_ref, keep_ref, got_ref, hold_ref, beside_ref, across_ref):
    x = lax.div(place_ref[0], NY)
    size = beside_ref.shape[1]
    for stream, (send_ref, near, far) in enumerate(
        ((beside_ref, beside, across), (across_ref, across, beside))
    ):
        rows = slice(stream * size, (stream + 1) * size)
        target = near(x)
        for slot, (stays, leaves) in enumerate(((x, target), (far(x), far(target)))):
            hold_ref[stream, slot] = keep_ref[stays, rows] + got_ref[stays, rows].astype(F32)
            total = keep_ref[leaves, rows] + got_ref[leaves, rows].astype(F32)
            send_ref[slot] = total.astype(BF16)


def halve_kernel(hold_ref, beside_ref, across_ref, own_ref, send_across_ref, send_beside_ref):
    for stream, (got_ref, send_ref) in enumerate(
        ((beside_ref, send_across_ref), (across_ref, send_beside_ref))
    ):
        own_ref[stream] = hold_ref[stream, 0] + got_ref[0].astype(F32)
        send_ref[...] = (hold_ref[stream, 1] + got_ref[1].astype(F32)).astype(BF16)


def leave_kernel(own_ref, across_ref, beside_ref, early_ref, late_ref, out_ref):
    peers, half, width = early_ref.shape
    out_ref[:, :half] = early_ref[...]
    out_ref[:, half:CELL] = late_ref[...]
    got = (across_ref[...].astype(F32), beside_ref[...].astype(F32))
    total = jnp.concatenate([(own_ref[n] + got[n]).astype(BF16) for n in range(2)])
    cell = total.shape[0] // peers

    def source_of(o):
        return jnp.where((o & 7) < cell, (o & 7) * peers + (o >> 3), -1)

    order = selection((peers * PAD, peers * cell), source_of)
    out_ref[:, CELL:] = reorder(order, total).reshape(peers, PAD, width)


def final_kernel(in_ref, received_ref, grads_ref):
    peers, _, width = in_ref.shape
    groups = peers // GROUP
    residues = peers * COLS
    span = GROUP * COLS

    def source_of(o):
        return ((o >> 2) & 15) * CELL + ((o >> 1) & 1) * 8 + (o >> 6) * HALF + (o & 1)

    order = selection((BLOCK, BLOCK), source_of)
    for g in range(groups):
        rows = in_ref[g * GROUP : (g + 1) * GROUP, :CELL].reshape(BLOCK, width)
        moved = reorder(order, rows)
        for i in range(ROWS):
            to = slice(i * residues + g * span, i * residues + (g + 1) * span)
            received_ref[to] = moved[i * span : (i + 1) * span]
    parts = in_ref[:, CELL:].astype(F32)
    quarters = NX
    parts = jnp.sum(parts.reshape(quarters, peers // quarters, PAD, width), axis=1)
    piece = grads_ref.shape[0] // quarters
    for q in range(quarters):
        for u in range(piece):
            grads_ref[q * piece + u] = parts[q, 2 * u : 2 * u + 2]


def shape(dims, dtype=BF16):
    return jax.ShapeDtypeStruct(dims, dtype)


def call(kernel, in_specs, out_shape, scratch=(), cost=(1e8, 1e6), mib=14):
    return pl.pallas_call(
        kernel,
        in_specs=in_specs,
        out_specs=jax.tree.map(lambda _: VMEM, out_shape),
        out_shape=out_shape,
        scratch_shapes=scratch,
        compiler_params=pltpu.CompilerParams(vmem_limit_bytes=mib * 1024 * 1024),
        cost_estimate=pl.CostEstimate(
            flops=int(cost[0]), bytes_accessed=int(cost[1]), transcendentals=0
        ),
    )


def exchange(array, groups=None):
    return lax.all_to_all(
        array, "mp", split_axis=0, concat_axis=0, axis_index_groups=groups, tiled=True
    )


def per_device(activations, out_grads, layer_weights):
    rows, residues, width = activations.shape[2:]
    peers = lax.axis_size("mp")
    tokens = rows * residues
    part = width // peers
    packed = call(
        pack_kernel,
        [HBM] * 2,
        shape((peers, 2 * CELL, width)),
        [pltpu.VMEM((2, tokens, width), BF16), pltpu.SemaphoreType.DMA((2,))],
        mib=56,
    )(
        activations.reshape(tokens, width), out_grads.reshape(tokens, width)
    )
    arrived = exchange(packed)
    weights = layer_weights[0]
    replica = lax.axis_index("dp").astype(jnp.int32).reshape(1)
    rows_held = tokens // 2
    back_shape = shape((peers, CELL // 2, width))
    held = [
        shape((rows_held, width)),
        shape((rows_held, width)),
        shape((rows_held, 3 * width)),
        shape((rows_held, width)),
    ]
    scratch = [pltpu.VMEM((rows_held, width), F32), pltpu.VMEM((rows_held, 4 * width), BF16)]
    cost = (2e9, 6e6)
    early, *kept = call(early_kernel, [VMEM] * 2, (back_shape, *held), scratch, cost)(
        arrived, weights
    )
    sections = lax.axis_size("section")

    def along(array):
        return lax.ppermute(array, "section", [(i + 1, i) for i in range(sections - 1)])

    early = along(early)
    terms_shape = (NX, 2 * width // NX, width)
    late, keep, give = call(
        late_kernel,
        [SMEM] + [VMEM] * 6,
        (back_shape, shape(terms_shape, F32), shape(terms_shape)),
        [
            *(pltpu.VMEM(one.shape, BF16) for one in held),
            *scratch,
            pltpu.VMEM((4, width // LANES, width, LANES), F32),
        ],
        cost,
    )(replica, arrived, weights, *kept)
    got = lax.ppermute(give, "dp", [(0, 1), (1, 0)])
    late = along(late)
    place = lax.axis_index("mp").astype(jnp.int32).reshape(1)
    size = width // NX

    def over_x(array, partner_of):
        pairs = [(q * NY + y, partner_of(q) * NY + y) for q in range(NX) for y in range(NY)]
        return lax.ppermute(array, "mp", pairs)

    def beside_of(q):
        return q ^ 1

    def across_of(q):
        return NX - 1 - q

    hold, near, far = call(
        spread_kernel,
        [SMEM] + [VMEM] * 2,
        (shape((2, 2, size, width), F32), *[shape((2, size, width))] * 2),
    )(place, keep, got)
    near = over_x(near, beside_of)
    far = over_x(far, across_of)
    own, far, near = call(
        halve_kernel,
        [VMEM] * 3,
        (shape((2, size, width), F32), *[shape((size, width))] * 2),
    )(hold, near, far)
    far = over_x(far, across_of)
    near = over_x(near, beside_of)
    leaving = call(leave_kernel, [VMEM] * 5, shape((peers, CELL + PAD, width)))(
        own, far, near, early, late
    )
    landed = exchange(leaving)
    received, weight_grads = call(
        final_kernel, [VMEM], (shape((tokens, width)), shape((part, 2, width), F32))
    )(landed)
    return (received.reshape(activations.shape), weight_grads.transpose(1, 0, 2)[None])


def solution(mesh):
    in_specs = (
        P("dp", "section", "mp", None, None),
        P("dp", "section", "mp", None, None),
        P("section", None, None, None),
    )
    out_specs = (P("dp", "section", "mp", None, None), P("section", "dp", "mp", None))

    return jax.shard_map(
        per_device, mesh=mesh, in_specs=in_specs, out_specs=out_specs, check_vma=False
    )
```

```python
import jax
import jax.numpy as jnp
import numpy as np
from jax import lax
from jax.experimental import pallas as pl
from jax.experimental.pallas import tpu as pltpu
from jax.sharding import PartitionSpec as P


HEAD_DIM = 64
EPS = 1e-05
F32 = jnp.float32
BF16 = jnp.bfloat16
LANES = 128
ROWS = 4
COLS = 4
CELL = ROWS * COLS
GROUP = 16
BLOCK = GROUP * CELL
NX = 4
PAD = 8
VMEM = pl.BlockSpec(memory_space=pltpu.VMEM)
SMEM = pl.BlockSpec(memory_space=pltpu.SMEM)


def dot(a, b, dims=((1,), (0,))):
    return lax.dot_general(a, b, (dims, ((), ())), preferred_element_type=F32)


def selection(size, source_of):
    out = lax.broadcasted_iota(jnp.int32, (size, size), 0)
    source = lax.broadcasted_iota(jnp.int32, (size, size), 1)
    return jnp.where(source_of(out) == source, 1.0, 0.0).astype(BF16)


def table(rows, columns, source_of):
    matrix = np.zeros((rows, columns), np.float32)
    for o in range(rows):
        if source_of(o) >= 0:
            matrix[o, source_of(o)] = 1.0
    return jnp.asarray(matrix, BF16)


def reorder(matrix, rows):
    return dot(matrix, rows).astype(BF16)


def pack_kernel(act_ref, grad_ref, out_ref, order_ref):
    @pl.when(pl.program_id(0) == 0)
    def _():
        order_ref[...] = selection(
            BLOCK, lambda o: ((o >> 2) & 3) * 64 + (o >> 4) * 4 + (o & 3)
        )

    for slot, ref in enumerate((act_ref, grad_ref)):
        moved = reorder(order_ref[...], ref[...].reshape(BLOCK, -1)).reshape(GROUP, CELL, -1)
        out_ref[:, slot * CELL : (slot + 1) * CELL] = moved


def attend_kernel(
    replica_ref,
    order_ref,
    in_ref,
    weight_ref,
    grads_ref,
    delta_ref,
    standard_ref,
    inverse_ref,
    keep_ref,
    give_ref,
    normed_ref,
    attn_ref,
    proj_ref,
):
    peers = in_ref.shape[0]
    groups = peers // GROUP
    width = in_ref.shape[2]
    seqs = peers * ROWS
    span = GROUP * ROWS
    order = order_ref[...]
    for g in range(groups):
        peers_of = slice(g * GROUP, (g + 1) * GROUP)
        acts = dot(order, in_ref[peers_of, :CELL].reshape(BLOCK, width))
        outs = reorder(order, in_ref[peers_of, CELL : 2 * CELL].reshape(BLOCK, width))
        for j in range(COLS):
            to = slice(j * seqs + g * span, j * seqs + (g + 1) * span)
            standard_ref[to] = acts[j * span : (j + 1) * span]
            delta_ref[to] = outs[j * span : (j + 1) * span]
    values = standard_ref[...]
    mean_value = jnp.mean(values, axis=-1, keepdims=True)
    centred = values - mean_value
    inverse = lax.rsqrt(jnp.mean(centred * centred, axis=-1, keepdims=True) + EPS)
    standard = centred * inverse
    standard_ref[...] = standard
    inverse_ref[...] = jnp.broadcast_to(inverse, inverse_ref.shape)
    normed = standard.astype(BF16)
    normed_ref[...] = normed
    joint = jnp.concatenate([weight_ref[n] for n in range(3)], axis=1)
    proj_ref[:, : 3 * width] = dot(normed, joint).astype(BF16)
    proj_ref[:, 3 * width :] = dot(delta_ref[...], weight_ref[3]).astype(BF16)

    scaling = HEAD_DIM ** (-0.5)
    low = lax.broadcasted_iota(jnp.int32, (seqs, LANES), 1) < HEAD_DIM

    def apart(pair):
        zero = jnp.zeros_like(pair)
        return jnp.concatenate([jnp.where(low, pair, zero), jnp.where(low, zero, pair)])

    def joined(columns):
        top, bottom = columns[:HEAD_DIM, :seqs], columns[HEAD_DIM:, seqs:]
        return jnp.concatenate([top, bottom]).astype(BF16).T

    def column(j, carry):
        here = pl.ds(pl.multiple_of(j * seqs, seqs), seqs)
        pairs = range(width // LANES)
        loaded = [
            [proj_ref[here, n * width + p * LANES : n * width + (p + 1) * LANES] for n in range(4)]
            for p in pairs
        ]
        split = [(apart(query), apart(delta)) for query, _, _, delta in loaded]
        scores = [dot(loaded[p][1], split[p][0], ((1,), (1,))) * scaling for p in pairs]
        dprobs = [dot(loaded[p][2], split[p][1], ((1,), (1,))) for p in pairs]
        for p in pairs:
            _, key, value, _ = loaded[p]
            queries, deltas = split[p]
            exponent = jnp.exp(scores[p] - jnp.max(scores[p], axis=0, keepdims=True))
            probs = exponent * (1.0 / jnp.sum(exponent, axis=0, keepdims=True))
            column_delta = jnp.sum(probs * dprobs[p], axis=0, keepdims=True)
            soft = probs.astype(BF16)
            dscores = (probs * (dprobs[p] - column_delta)).astype(BF16)
            lanes = [slice(n * width + p * LANES, n * width + (p + 1) * LANES) for n in range(3)]
            attn_ref[here, lanes[0]] = joined(dot(value, soft, ((0,), (0,))))
            grads_ref[here, lanes[0]] = joined(dot(key, dscores, ((0,), (0,))) * scaling)
            grads_ref[here, lanes[1]] = (dot(dscores, queries) * scaling).astype(BF16)
            grads_ref[here, lanes[2]] = dot(soft, deltas).astype(BF16)
        return carry

    lax.fori_loop(0, COLS, column, 0, unroll=4)

    first = replica_ref[0] == 0
    term = dot(normed_ref[...], grads_ref[...], ((0,), (0,)))
    terms = [term[:, n * width : (n + 1) * width] for n in range(3)]
    terms.append(dot(delta_ref[...], attn_ref[...], ((0,), (0,))))
    for m in range(2):
        keep_ref[m] = jnp.where(first, terms[m], terms[m + 2])
        give_ref[m] = jnp.where(first, terms[m + 2], terms[m]).astype(BF16)


def input_kernel(order_ref, grads_ref, delta_ref, standard_ref, inverse_ref, weight_ref, back_ref):
    groups = back_ref.shape[0] // GROUP
    tokens, width = delta_ref.shape
    seqs = tokens // COLS
    span = GROUP * ROWS
    joint = jnp.concatenate([weight_ref[n] for n in range(3)], axis=1)
    grad_in = dot(grads_ref[...], joint, ((1,), (1,)))
    standard = standard_ref[...]
    grad_mean = jnp.mean(grad_in, axis=-1, keepdims=True)
    grad_proj = jnp.mean(grad_in * standard, axis=-1, keepdims=True)
    branch = inverse_ref[:, :1] * (grad_in - grad_mean - standard * grad_proj)
    branch = branch.astype(BF16).astype(F32)
    input_grad = (delta_ref[...].astype(F32) + branch).astype(BF16)
    order = order_ref[...]
    for g in range(groups):
        rows = jnp.concatenate(
            [input_grad[j * seqs + g * span : j * seqs + (g + 1) * span] for j in range(COLS)]
        )
        back_ref[g * GROUP : (g + 1) * GROUP] = reorder(order, rows).reshape(GROUP, CELL, width)


def spread_kernel(order_ref, keep_ref, got_ref, out_ref):
    quarters = out_ref.shape[0]
    block = order_ref.shape[0] // 2
    size = 2 * block // quarters
    for g in range(keep_ref.shape[1] // block):
        here = slice(g * block, (g + 1) * block)
        rows = [(keep_ref[m, here] + got_ref[m, here].astype(F32)).astype(BF16) for m in range(2)]
        moved = reorder(order_ref[...], jnp.concatenate(rows))
        for q in range(quarters):
            out_ref[q, g * size : (g + 1) * size] = moved[q * size : (q + 1) * size]


def leave_kernel(order_ref, parts_ref, back_ref, out_ref):
    peers, _, width = back_ref.shape
    out_ref[:, :CELL] = back_ref[...]
    total = jnp.sum(parts_ref[...].astype(F32), axis=0).astype(BF16)
    out_ref[:, CELL:] = reorder(order_ref[...], total).reshape(peers, PAD, width)


def final_kernel(order_ref, in_ref, received_ref, grads_ref):
    peers, _, width = in_ref.shape
    groups = peers // GROUP
    residues = peers * COLS
    span = GROUP * COLS
    order = order_ref[...]
    for g in range(groups):
        rows = in_ref[g * GROUP : (g + 1) * GROUP, :CELL].reshape(BLOCK, width)
        moved = reorder(order, rows)
        for i in range(ROWS):
            to = slice(i * residues + g * span, i * residues + (g + 1) * span)
            received_ref[to] = moved[i * span : (i + 1) * span]
    parts = in_ref[:, CELL:].astype(F32)
    quarters = NX
    parts = jnp.sum(parts.reshape(quarters, peers // quarters, PAD, width), axis=1)
    piece = grads_ref.shape[0] // quarters
    for q in range(quarters):
        for u in range(piece):
            grads_ref[q * piece + u] = parts[q, 2 * u : 2 * u + 2]


def shape(dims, dtype=BF16):
    return jax.ShapeDtypeStruct(dims, dtype)


def call(kernel, in_specs, out_shape, scratch=(), cost=(1e8, 1e6)):
    return pl.pallas_call(
        kernel,
        in_specs=in_specs,
        out_specs=jax.tree.map(lambda _: VMEM, out_shape),
        out_shape=out_shape,
        scratch_shapes=scratch,
        compiler_params=pltpu.CompilerParams(vmem_limit_bytes=14 * 1024 * 1024),
        cost_estimate=pl.CostEstimate(
            flops=int(cost[0]), bytes_accessed=int(cost[1]), transcendentals=0
        ),
    )


def exchange(array, groups=None):
    return lax.all_to_all(
        array, "mp", split_axis=0, concat_axis=0, axis_index_groups=groups, tiled=True
    )


def per_device(activations, out_grads, layer_weights):
    rows, residues, width = activations.shape[2:]
    peers = lax.axis_size("mp")
    tokens = rows * residues
    part = width // peers
    groups = peers // GROUP
    span = GROUP * COLS
    taken = pl.BlockSpec((rows, 1, span, width), lambda g: (0, g, 0, 0))
    packed = pl.pallas_call(
        pack_kernel,
        grid=(groups,),
        in_specs=[taken] * 2,
        out_specs=pl.BlockSpec((GROUP, 2 * CELL, width), lambda g: (g, 0, 0)),
        out_shape=shape((peers, 2 * CELL, width)),
        scratch_shapes=[pltpu.VMEM((BLOCK, BLOCK), BF16)],
        compiler_params=pltpu.CompilerParams(vmem_limit_bytes=56 * 1024 * 1024),
    )(
        activations.reshape(rows, groups, span, width),
        out_grads.reshape(rows, groups, span, width),
    )
    arrived = exchange(packed)
    weights = layer_weights[0]
    replica = lax.axis_index("dp").astype(jnp.int32).reshape(1)
    grads, delta, standard, inverse, keep, give = call(
        attend_kernel,
        [SMEM] + [VMEM] * 3,
        (
            shape((tokens, 3 * width)),
            shape((tokens, width)),
            shape((tokens, width), F32),
            shape((tokens, LANES), F32),
            shape((2, width, width), F32),
            shape((2, width, width)),
        ),
        [
            pltpu.VMEM((tokens, width), BF16),
            pltpu.VMEM((tokens, width), BF16),
            pltpu.VMEM((tokens, 4 * width), BF16),
        ],
        cost=(3e9, 9e6),
    )(
        replica,
        table(BLOCK, BLOCK, lambda o: ((o >> 2) & 15) * 16 + (o & 3) * 4 + (o >> 6)),
        arrived,
        weights,
    )
    got = lax.ppermute(give, "dp", [(0, 1), (1, 0)])
    order = table(BLOCK, BLOCK, lambda o: (o & 3) * 64 + (o >> 4) * 4 + ((o >> 2) & 3))
    back = call(input_kernel, [VMEM] * 6, shape((peers, CELL, width)), cost=(1e9, 3e6))(
        order, grads, delta, standard, inverse, weights
    )
    keep, back = lax.optimization_barrier((keep, back))
    sections = lax.axis_size("section")
    back = lax.ppermute(back, "section", [(i + 1, i) for i in range(sections - 1)])
    piece = part // NX

    def spread_from(o):
        quarter, rest = divmod(o, 16 * piece)
        device, inside = divmod(rest, 2 * piece)
        return (inside & 1) * 8 * part + device * part + quarter * piece + (inside >> 1)

    spread = call(
        spread_kernel, [VMEM] * 3, shape((NX, 2 * width // NX, width)), cost=(1e9, 3e6)
    )(table(16 * part, 16 * part, spread_from), keep, got)
    ny = peers // NX
    groups = [[x * ny + y for x in range(NX)] for y in range(ny)]
    parts = exchange(spread, groups)
    cell = 2 * piece
    order = table(
        peers * PAD, peers * cell, lambda o: (o >> 3) * cell + (o & 7) if (o & 7) < cell else -1
    )
    leaving = call(leave_kernel, [VMEM] * 3, shape((peers, CELL + PAD, width)))(order, parts, back)
    landed = exchange(leaving)
    received, weight_grads = call(
        final_kernel, [VMEM] * 2, (shape((tokens, width)), shape((part, 2, width), F32))
    )(
        table(BLOCK, BLOCK, lambda o: ((o >> 2) & 15) * 16 + (o >> 6) * 4 + (o & 3)),
        landed,
    )
    return (received.reshape(activations.shape), weight_grads.transpose(1, 0, 2)[None])


def solution(mesh):
    in_specs = (
        P("dp", "section", "mp", None, None),
        P("dp", "section", "mp", None, None),
        P("section", None, None, None),
    )
    out_specs = (P("dp", "section", "mp", None, None), P("section", "dp", "mp", None))

    return jax.shard_map(
        per_device, mesh=mesh, in_specs=in_specs, out_specs=out_specs, check_vma=False
    )
```

```python
import jax
import jax.numpy as jnp
import numpy as np
from jax import lax
from jax.experimental import pallas as pl
from jax.experimental.pallas import tpu as pltpu
from jax.sharding import PartitionSpec as P


HEAD_DIM = 64
EPS = 1e-05
F32 = jnp.float32
BF16 = jnp.bfloat16
LANES = 128
ROWS = 4
COLS = 4
CELL = ROWS * COLS
GROUP = 16
BLOCK = GROUP * CELL
NX = 4
PAD = 8
VMEM = pl.BlockSpec(memory_space=pltpu.VMEM)
SMEM = pl.BlockSpec(memory_space=pltpu.SMEM)


def dot(a, b, dims=((1,), (0,))):
    return lax.dot_general(a, b, (dims, ((), ())), preferred_element_type=F32)


def selection(size, source_of):
    out = lax.broadcasted_iota(jnp.int32, (size, size), 0)
    source = lax.broadcasted_iota(jnp.int32, (size, size), 1)
    return jnp.where(source_of(out) == source, 1.0, 0.0).astype(BF16)


def table(rows, columns, source_of):
    matrix = np.zeros((rows, columns), np.float32)
    for o in range(rows):
        if source_of(o) >= 0:
            matrix[o, source_of(o)] = 1.0
    return jnp.asarray(matrix, BF16)


def reorder(matrix, rows):
    return dot(matrix, rows).astype(BF16)


def pack_kernel(_, act_ref, grad_ref, out_ref, order_ref):
    @pl.when(pl.program_id(0) == 0)
    def _():
        order_ref[...] = selection(
            BLOCK, lambda o: ((o >> 2) & 3) * 64 + (o >> 4) * 4 + (o & 3)
        )

    for slot, ref in enumerate((act_ref, grad_ref)):
        moved = reorder(order_ref[...], ref[...].reshape(BLOCK, -1)).reshape(GROUP, CELL, -1)
        out_ref[:, slot * CELL : (slot + 1) * CELL] = moved


def attend_kernel(
    replica_ref,
    order_ref,
    in_ref,
    weight_ref,
    grads_ref,
    delta_ref,
    standard_ref,
    inverse_ref,
    keep_ref,
    give_ref,
    normed_ref,
    attn_ref,
    proj_ref,
):
    peers = in_ref.shape[0]
    groups = peers // GROUP
    width = in_ref.shape[2]
    seqs = peers * ROWS
    span = GROUP * ROWS
    order = order_ref[...]
    for g in range(groups):
        peers_of = slice(g * GROUP, (g + 1) * GROUP)
        acts = dot(order, in_ref[peers_of, :CELL].reshape(BLOCK, width))
        outs = reorder(order, in_ref[peers_of, CELL : 2 * CELL].reshape(BLOCK, width))
        for j in range(COLS):
            to = slice(j * seqs + g * span, j * seqs + (g + 1) * span)
            standard_ref[to] = acts[j * span : (j + 1) * span]
            delta_ref[to] = outs[j * span : (j + 1) * span]
    values = standard_ref[...]
    mean_value = jnp.mean(values, axis=-1, keepdims=True)
    centred = values - mean_value
    inverse = lax.rsqrt(jnp.mean(centred * centred, axis=-1, keepdims=True) + EPS)
    standard = centred * inverse
    standard_ref[...] = standard
    inverse_ref[...] = jnp.broadcast_to(inverse, inverse_ref.shape)
    normed = standard.astype(BF16)
    normed_ref[...] = normed
    joint = jnp.concatenate([weight_ref[n] for n in range(3)], axis=1)
    proj_ref[:, : 3 * width] = dot(normed, joint).astype(BF16)
    proj_ref[:, 3 * width :] = dot(delta_ref[...], weight_ref[3]).astype(BF16)

    scaling = HEAD_DIM ** (-0.5)
    low = lax.broadcasted_iota(jnp.int32, (seqs, LANES), 1) < HEAD_DIM

    def apart(pair):
        zero = jnp.zeros_like(pair)
        return jnp.concatenate([jnp.where(low, pair, zero), jnp.where(low, zero, pair)])

    def joined(columns):
        top, bottom = columns[:HEAD_DIM, :seqs], columns[HEAD_DIM:, seqs:]
        return jnp.concatenate([top, bottom]).astype(BF16).T

    def column(j, carry):
        here = pl.ds(pl.multiple_of(j * seqs, seqs), seqs)
        pairs = range(width // LANES)
        loaded = [
            [proj_ref[here, n * width + p * LANES : n * width + (p + 1) * LANES] for n in range(4)]
            for p in pairs
        ]
        split = [(apart(query), apart(delta)) for query, _, _, delta in loaded]
        scores = [dot(loaded[p][1], split[p][0], ((1,), (1,))) * scaling for p in pairs]
        dprobs = [dot(loaded[p][2], split[p][1], ((1,), (1,))) for p in pairs]
        for p in pairs:
            _, key, value, _ = loaded[p]
            queries, deltas = split[p]
            exponent = jnp.exp(scores[p] - jnp.max(scores[p], axis=0, keepdims=True))
            probs = exponent * (1.0 / jnp.sum(exponent, axis=0, keepdims=True))
            column_delta = jnp.sum(probs * dprobs[p], axis=0, keepdims=True)
            soft = probs.astype(BF16)
            dscores = (probs * (dprobs[p] - column_delta)).astype(BF16)
            lanes = [slice(n * width + p * LANES, n * width + (p + 1) * LANES) for n in range(3)]
            attn_ref[here, lanes[0]] = joined(dot(value, soft, ((0,), (0,))))
            grads_ref[here, lanes[0]] = joined(dot(key, dscores, ((0,), (0,))) * scaling)
            grads_ref[here, lanes[1]] = (dot(dscores, queries) * scaling).astype(BF16)
            grads_ref[here, lanes[2]] = dot(soft, deltas).astype(BF16)
        return carry

    lax.fori_loop(0, COLS, column, 0, unroll=4)

    first = replica_ref[0] == 0
    term = dot(normed_ref[...], grads_ref[...], ((0,), (0,)))
    terms = [term[:, n * width : (n + 1) * width] for n in range(3)]
    terms.append(dot(delta_ref[...], attn_ref[...], ((0,), (0,))))
    for m in range(2):
        keep_ref[m] = jnp.where(first, terms[m], terms[m + 2])
        give_ref[m] = jnp.where(first, terms[m + 2], terms[m]).astype(BF16)


def input_kernel(order_ref, grads_ref, delta_ref, standard_ref, inverse_ref, weight_ref, back_ref):
    groups = back_ref.shape[0] // GROUP
    tokens, width = delta_ref.shape
    seqs = tokens // COLS
    span = GROUP * ROWS
    joint = jnp.concatenate([weight_ref[n] for n in range(3)], axis=1)
    grad_in = dot(grads_ref[...], joint, ((1,), (1,)))
    standard = standard_ref[...]
    grad_mean = jnp.mean(grad_in, axis=-1, keepdims=True)
    grad_proj = jnp.mean(grad_in * standard, axis=-1, keepdims=True)
    branch = inverse_ref[:, :1] * (grad_in - grad_mean - standard * grad_proj)
    branch = branch.astype(BF16).astype(F32)
    input_grad = (delta_ref[...].astype(F32) + branch).astype(BF16)
    order = order_ref[...]
    for g in range(groups):
        rows = jnp.concatenate(
            [input_grad[j * seqs + g * span : j * seqs + (g + 1) * span] for j in range(COLS)]
        )
        back_ref[g * GROUP : (g + 1) * GROUP] = reorder(order, rows).reshape(GROUP, CELL, width)


def spread_kernel(order_ref, keep_ref, got_ref, out_ref):
    quarters = out_ref.shape[0]
    block = order_ref.shape[0] // 2
    size = 2 * block // quarters
    for g in range(keep_ref.shape[1] // block):
        here = slice(g * block, (g + 1) * block)
        rows = [(keep_ref[m, here] + got_ref[m, here].astype(F32)).astype(BF16) for m in range(2)]
        moved = reorder(order_ref[...], jnp.concatenate(rows))
        for q in range(quarters):
            out_ref[q, g * size : (g + 1) * size] = moved[q * size : (q + 1) * size]


def collect_kernel(order_ref, parts_ref, out_ref):
    total = jnp.sum(parts_ref[...].astype(F32), axis=0).astype(BF16)
    out_ref[...] = reorder(order_ref[...], total).reshape(out_ref.shape)


def leave_kernel(back_ref, cells_ref, out_ref):
    out_ref[:, :CELL] = back_ref[...]
    out_ref[:, CELL:] = cells_ref[...]


def final_kernel(order_ref, in_ref, received_ref, grads_ref):
    peers, _, width = in_ref.shape
    groups = peers // GROUP
    residues = peers * COLS
    span = GROUP * COLS
    order = order_ref[...]
    for g in range(groups):
        rows = in_ref[g * GROUP : (g + 1) * GROUP, :CELL].reshape(BLOCK, width)
        moved = reorder(order, rows)
        for i in range(ROWS):
            to = slice(i * residues + g * span, i * residues + (g + 1) * span)
            received_ref[to] = moved[i * span : (i + 1) * span]
    parts = in_ref[:, CELL:].astype(F32)
    quarters = NX
    parts = jnp.sum(parts.reshape(quarters, peers // quarters, PAD, width), axis=1)
    piece = grads_ref.shape[0] // quarters
    for q in range(quarters):
        for u in range(piece):
            grads_ref[q * piece + u] = parts[q, 2 * u : 2 * u + 2]


def shape(dims, dtype=BF16):
    return jax.ShapeDtypeStruct(dims, dtype)


def call(kernel, in_specs, out_shape, scratch=(), cost=(1e8, 1e6)):
    return pl.pallas_call(
        kernel,
        in_specs=in_specs,
        out_specs=jax.tree.map(lambda _: VMEM, out_shape),
        out_shape=out_shape,
        scratch_shapes=scratch,
        compiler_params=pltpu.CompilerParams(vmem_limit_bytes=14 * 1024 * 1024),
        cost_estimate=pl.CostEstimate(
            flops=int(cost[0]), bytes_accessed=int(cost[1]), transcendentals=0
        ),
    )


def exchange(array, groups=None):
    return lax.all_to_all(
        array, "mp", split_axis=0, concat_axis=0, axis_index_groups=groups, tiled=True
    )


def per_device(activations, out_grads, layer_weights):
    rows, residues, width = activations.shape[2:]
    peers = lax.axis_size("mp")
    tokens = rows * residues
    part = width // peers
    replica = lax.axis_index("dp").astype(jnp.int32).reshape(1)
    groups = peers // GROUP
    span = GROUP * COLS
    taken = pl.BlockSpec((rows, 1, span, width), lambda g: (0, g, 0, 0))
    packed = pl.pallas_call(
        pack_kernel,
        grid=(groups,),
        in_specs=[SMEM] + [taken] * 2,
        out_specs=pl.BlockSpec((GROUP, 2 * CELL, width), lambda g: (g, 0, 0)),
        out_shape=shape((peers, 2 * CELL, width)),
        scratch_shapes=[pltpu.VMEM((BLOCK, BLOCK), BF16)],
        compiler_params=pltpu.CompilerParams(vmem_limit_bytes=56 * 1024 * 1024),
    )(
        replica,
        activations.reshape(rows, groups, span, width),
        out_grads.reshape(rows, groups, span, width),
    )
    arrived = exchange(packed)
    weights = layer_weights[0]
    grads, delta, standard, inverse, keep, give = call(
        attend_kernel,
        [SMEM] + [VMEM] * 3,
        (
            shape((tokens, 3 * width)),
            shape((tokens, width)),
            shape((tokens, width), F32),
            shape((tokens, LANES), F32),
            shape((2, width, width), F32),
            shape((2, width, width)),
        ),
        [
            pltpu.VMEM((tokens, width), BF16),
            pltpu.VMEM((tokens, width), BF16),
            pltpu.VMEM((tokens, 4 * width), BF16),
        ],
        cost=(3e9, 9e6),
    )(
        replica,
        table(BLOCK, BLOCK, lambda o: ((o >> 2) & 15) * 16 + (o & 3) * 4 + (o >> 6)),
        arrived,
        weights,
    )
    got = lax.ppermute(give, "dp", [(0, 1), (1, 0)])
    order = table(BLOCK, BLOCK, lambda o: (o & 3) * 64 + (o >> 4) * 4 + ((o >> 2) & 3))
    back = call(input_kernel, [VMEM] * 6, shape((peers, CELL, width)), cost=(1e9, 3e6))(
        order, grads, delta, standard, inverse, weights
    )
    keep, back = lax.optimization_barrier((keep, back))
    sections = lax.axis_size("section")
    back = lax.ppermute(back, "section", [(i + 1, i) for i in range(sections - 1)])
    piece = part // NX

    def spread_from(o):
        quarter, rest = divmod(o, 16 * piece)
        device, inside = divmod(rest, 2 * piece)
        return (inside & 1) * 8 * part + device * part + quarter * piece + (inside >> 1)

    spread = call(
        spread_kernel, [VMEM] * 3, shape((NX, 2 * width // NX, width)), cost=(1e9, 3e6)
    )(table(16 * part, 16 * part, spread_from), keep, got)
    ny = peers // NX
    groups = [[x * ny + y for x in range(NX)] for y in range(ny)]
    parts = exchange(spread, groups)
    cell = 2 * piece
    order = table(
        peers * PAD, peers * cell, lambda o: (o >> 3) * cell + (o & 7) if (o & 7) < cell else -1
    )
    cells = call(collect_kernel, [VMEM] * 2, shape((peers, PAD, width)))(order, parts)
    leaving = call(leave_kernel, [VMEM] * 2, shape((peers, CELL + PAD, width)))(back, cells)
    landed = exchange(leaving)
    received, weight_grads = call(
        final_kernel, [VMEM] * 2, (shape((tokens, width)), shape((part, 2, width), F32))
    )(
        table(BLOCK, BLOCK, lambda o: ((o >> 2) & 15) * 16 + (o >> 6) * 4 + (o & 3)),
        landed,
    )
    return (received.reshape(activations.shape), weight_grads.transpose(1, 0, 2)[None])


def solution(mesh):
    in_specs = (
        P("dp", "section", "mp", None, None),
        P("dp", "section", "mp", None, None),
        P("section", None, None, None),
    )
    out_specs = (P("dp", "section", "mp", None, None), P("section", "dp", "mp", None))

    return jax.shard_map(
        per_device, mesh=mesh, in_specs=in_specs, out_specs=out_specs, check_vma=False
    )
```

```python
import jax
import jax.numpy as jnp
import numpy as np
from jax import lax
from jax.experimental import pallas as pl
from jax.experimental.pallas import tpu as pltpu
from jax.sharding import PartitionSpec as P


HEAD_DIM = 64
EPS = 1e-05
F32 = jnp.float32
BF16 = jnp.bfloat16
LANES = 128
ROWS = 4
COLS = 4
CELL = ROWS * COLS
GROUP = 16
BLOCK = GROUP * CELL
NX = 4
PAD = 8
VMEM = pl.BlockSpec(memory_space=pltpu.VMEM)
SMEM = pl.BlockSpec(memory_space=pltpu.SMEM)


def dot(a, b, dims=((1,), (0,))):
    return lax.dot_general(a, b, (dims, ((), ())), preferred_element_type=F32)


def selection(size, source_of):
    out = lax.broadcasted_iota(jnp.int32, (size, size), 0)
    source = lax.broadcasted_iota(jnp.int32, (size, size), 1)
    return jnp.where(source_of(out) == source, 1.0, 0.0).astype(BF16)


def table(rows, columns, source_of):
    matrix = np.zeros((rows, columns), np.float32)
    for o in range(rows):
        if source_of(o) >= 0:
            matrix[o, source_of(o)] = 1.0
    return jnp.asarray(matrix, BF16)


def reorder(matrix, rows):
    return dot(matrix, rows).astype(BF16)


def pack_kernel(_, act_ref, grad_ref, out_ref, order_ref):
    @pl.when(pl.program_id(0) == 0)
    def _():
        order_ref[...] = selection(
            BLOCK, lambda o: ((o >> 2) & 3) * 64 + (o >> 4) * 4 + (o & 3)
        )

    for slot, ref in enumerate((act_ref, grad_ref)):
        moved = reorder(order_ref[...], ref[...].reshape(BLOCK, -1)).reshape(GROUP, CELL, -1)
        out_ref[:, slot * CELL : (slot + 1) * CELL] = moved


def attend_kernel(
    replica_ref,
    order_ref,
    back_order_ref,
    in_ref,
    weight_ref,
    back_ref,
    keep_ref,
    give_ref,
    grads_ref,
    delta_ref,
    standard_ref,
    normed_ref,
    attn_ref,
    proj_ref,
):
    peers = in_ref.shape[0]
    groups = peers // GROUP
    width = in_ref.shape[2]
    seqs = peers * ROWS
    span = GROUP * ROWS
    order = order_ref[...]
    for g in range(groups):
        peers_of = slice(g * GROUP, (g + 1) * GROUP)
        acts = dot(order, in_ref[peers_of, :CELL].reshape(BLOCK, width))
        outs = reorder(order, in_ref[peers_of, CELL : 2 * CELL].reshape(BLOCK, width))
        for j in range(COLS):
            to = slice(j * seqs + g * span, j * seqs + (g + 1) * span)
            standard_ref[to] = acts[j * span : (j + 1) * span]
            delta_ref[to] = outs[j * span : (j + 1) * span]
    values = standard_ref[...]
    mean_value = jnp.mean(values, axis=-1, keepdims=True)
    centred = values - mean_value
    inverse = lax.rsqrt(jnp.mean(centred * centred, axis=-1, keepdims=True) + EPS)
    standard = centred * inverse
    standard_ref[...] = standard
    normed = standard.astype(BF16)
    normed_ref[...] = normed
    joint = jnp.concatenate([weight_ref[n] for n in range(3)], axis=1)
    proj_ref[:, : 3 * width] = dot(normed, joint).astype(BF16)
    proj_ref[:, 3 * width :] = dot(delta_ref[...], weight_ref[3]).astype(BF16)

    scaling = HEAD_DIM ** (-0.5)
    low = lax.broadcasted_iota(jnp.int32, (seqs, LANES), 1) < HEAD_DIM

    def apart(pair):
        zero = jnp.zeros_like(pair)
        return jnp.concatenate([jnp.where(low, pair, zero), jnp.where(low, zero, pair)])

    def joined(columns):
        top, bottom = columns[:HEAD_DIM, :seqs], columns[HEAD_DIM:, seqs:]
        return jnp.concatenate([top, bottom]).astype(BF16).T

    def column(j, carry):
        here = pl.ds(pl.multiple_of(j * seqs, seqs), seqs)
        pairs = range(width // LANES)
        loaded = [
            [proj_ref[here, n * width + p * LANES : n * width + (p + 1) * LANES] for n in range(4)]
            for p in pairs
        ]
        split = [(apart(query), apart(delta)) for query, _, _, delta in loaded]
        scores = [dot(loaded[p][1], split[p][0], ((1,), (1,))) * scaling for p in pairs]
        dprobs = [dot(loaded[p][2], split[p][1], ((1,), (1,))) for p in pairs]
        for p in pairs:
            _, key, value, _ = loaded[p]
            queries, deltas = split[p]
            exponent = jnp.exp(scores[p] - jnp.max(scores[p], axis=0, keepdims=True))
            probs = exponent * (1.0 / jnp.sum(exponent, axis=0, keepdims=True))
            column_delta = jnp.sum(probs * dprobs[p], axis=0, keepdims=True)
            soft = probs.astype(BF16)
            dscores = (probs * (dprobs[p] - column_delta)).astype(BF16)
            lanes = [slice(n * width + p * LANES, n * width + (p + 1) * LANES) for n in range(3)]
            attn_ref[here, lanes[0]] = joined(dot(value, soft, ((0,), (0,))))
            grads_ref[here, lanes[0]] = joined(dot(key, dscores, ((0,), (0,))) * scaling)
            grads_ref[here, lanes[1]] = (dot(dscores, queries) * scaling).astype(BF16)
            grads_ref[here, lanes[2]] = dot(soft, deltas).astype(BF16)
        return carry

    lax.fori_loop(0, COLS, column, 0, unroll=4)

    grad_in = dot(grads_ref[...], joint, ((1,), (1,)))
    standard = standard_ref[...]
    grad_mean = jnp.mean(grad_in, axis=-1, keepdims=True)
    grad_proj = jnp.mean(grad_in * standard, axis=-1, keepdims=True)
    branch = inverse * (grad_in - grad_mean - standard * grad_proj)
    branch = branch.astype(BF16).astype(F32)
    input_grad = (delta_ref[...].astype(F32) + branch).astype(BF16)
    order = back_order_ref[...]
    for g in range(groups):
        rows = jnp.concatenate(
            [input_grad[j * seqs + g * span : j * seqs + (g + 1) * span] for j in range(COLS)]
        )
        back_ref[g * GROUP : (g + 1) * GROUP] = reorder(order, rows).reshape(GROUP, CELL, width)

    first = replica_ref[0] == 0
    term = dot(normed_ref[...], grads_ref[...], ((0,), (0,)))
    terms = [term[:, n * width : (n + 1) * width] for n in range(3)]
    terms.append(dot(delta_ref[...], attn_ref[...], ((0,), (0,))))
    for m in range(2):
        keep_ref[m] = jnp.where(first, terms[m], terms[m + 2])
        give_ref[m] = jnp.where(first, terms[m + 2], terms[m]).astype(BF16)


def spread_kernel(order_ref, keep_ref, got_ref, out_ref):
    quarters = out_ref.shape[0]
    block = order_ref.shape[0] // 2
    size = 2 * block // quarters
    for g in range(keep_ref.shape[1] // block):
        here = slice(g * block, (g + 1) * block)
        rows = [(keep_ref[m, here] + got_ref[m, here].astype(F32)).astype(BF16) for m in range(2)]
        moved = reorder(order_ref[...], jnp.concatenate(rows))
        for q in range(quarters):
            out_ref[q, g * size : (g + 1) * size] = moved[q * size : (q + 1) * size]


def collect_kernel(order_ref, parts_ref, out_ref):
    total = jnp.sum(parts_ref[...].astype(F32), axis=0).astype(BF16)
    out_ref[...] = reorder(order_ref[...], total).reshape(out_ref.shape)


def leave_kernel(back_ref, cells_ref, out_ref):
    out_ref[:, :CELL] = back_ref[...]
    out_ref[:, CELL:] = cells_ref[...]


def final_kernel(order_ref, in_ref, received_ref, grads_ref):
    peers, _, width = in_ref.shape
    groups = peers // GROUP
    residues = peers * COLS
    span = GROUP * COLS
    order = order_ref[...]
    for g in range(groups):
        rows = in_ref[g * GROUP : (g + 1) * GROUP, :CELL].reshape(BLOCK, width)
        moved = reorder(order, rows)
        for i in range(ROWS):
            to = slice(i * residues + g * span, i * residues + (g + 1) * span)
            received_ref[to] = moved[i * span : (i + 1) * span]
    parts = in_ref[:, CELL:].astype(F32)
    quarters = NX
    parts = jnp.sum(parts.reshape(quarters, peers // quarters, PAD, width), axis=1)
    piece = grads_ref.shape[0] // quarters
    for q in range(quarters):
        for u in range(piece):
            grads_ref[q * piece + u] = parts[q, 2 * u : 2 * u + 2]


def shape(dims, dtype=BF16):
    return jax.ShapeDtypeStruct(dims, dtype)


def call(kernel, in_specs, out_shape, scratch=(), cost=(1e8, 1e6)):
    return pl.pallas_call(
        kernel,
        in_specs=in_specs,
        out_specs=jax.tree.map(lambda _: VMEM, out_shape),
        out_shape=out_shape,
        scratch_shapes=scratch,
        compiler_params=pltpu.CompilerParams(vmem_limit_bytes=14 * 1024 * 1024),
        cost_estimate=pl.CostEstimate(
            flops=int(cost[0]), bytes_accessed=int(cost[1]), transcendentals=0
        ),
    )


def exchange(array, groups=None):
    return lax.all_to_all(
        array, "mp", split_axis=0, concat_axis=0, axis_index_groups=groups, tiled=True
    )


def per_device(activations, out_grads, layer_weights):
    rows, residues, width = activations.shape[2:]
    peers = lax.axis_size("mp")
    tokens = rows * residues
    part = width // peers
    replica = lax.axis_index("dp").astype(jnp.int32).reshape(1)
    groups = peers // GROUP
    span = GROUP * COLS
    taken = pl.BlockSpec((rows, 1, span, width), lambda g: (0, g, 0, 0))
    packed = pl.pallas_call(
        pack_kernel,
        grid=(groups,),
        in_specs=[SMEM] + [taken] * 2,
        out_specs=pl.BlockSpec((GROUP, 2 * CELL, width), lambda g: (g, 0, 0)),
        out_shape=shape((peers, 2 * CELL, width)),
        scratch_shapes=[pltpu.VMEM((BLOCK, BLOCK), BF16)],
        compiler_params=pltpu.CompilerParams(vmem_limit_bytes=56 * 1024 * 1024),
    )(
        replica,
        activations.reshape(rows, groups, span, width),
        out_grads.reshape(rows, groups, span, width),
    )
    arrived = exchange(packed)
    weights = layer_weights[0]
    back, keep, give = call(
        attend_kernel,
        [SMEM] + [VMEM] * 4,
        (
            shape((peers, CELL, width)),
            shape((2, width, width), F32),
            shape((2, width, width)),
        ),
        [
            pltpu.VMEM((tokens, 3 * width), BF16),
            pltpu.VMEM((tokens, width), BF16),
            pltpu.VMEM((tokens, width), F32),
            pltpu.VMEM((tokens, width), BF16),
            pltpu.VMEM((tokens, width), BF16),
            pltpu.VMEM((tokens, 4 * width), BF16),
        ],
        cost=(4e9, 9e6),
    )(
        replica,
        table(BLOCK, BLOCK, lambda o: ((o >> 2) & 15) * 16 + (o & 3) * 4 + (o >> 6)),
        table(BLOCK, BLOCK, lambda o: (o & 3) * 64 + (o >> 4) * 4 + ((o >> 2) & 3)),
        arrived,
        weights,
    )
    got = lax.ppermute(give, "dp", [(0, 1), (1, 0)])
    sections = lax.axis_size("section")
    back = lax.ppermute(back, "section", [(i + 1, i) for i in range(sections - 1)])
    piece = part // NX

    def spread_from(o):
        quarter, rest = divmod(o, 16 * piece)
        device, inside = divmod(rest, 2 * piece)
        return (inside & 1) * 8 * part + device * part + quarter * piece + (inside >> 1)

    spread = call(
        spread_kernel, [VMEM] * 3, shape((NX, 2 * width // NX, width)), cost=(1e9, 3e6)
    )(table(16 * part, 16 * part, spread_from), keep, got)
    ny = peers // NX
    groups = [[x * ny + y for x in range(NX)] for y in range(ny)]
    parts = exchange(spread, groups)
    cell = 2 * piece
    order = table(
        peers * PAD, peers * cell, lambda o: (o >> 3) * cell + (o & 7) if (o & 7) < cell else -1
    )
    cells = call(collect_kernel, [VMEM] * 2, shape((peers, PAD, width)))(order, parts)
    leaving = call(leave_kernel, [VMEM] * 2, shape((peers, CELL + PAD, width)))(back, cells)
    landed = exchange(leaving)
    received, weight_grads = call(
        final_kernel, [VMEM] * 2, (shape((tokens, width)), shape((part, 2, width), F32))
    )(
        table(BLOCK, BLOCK, lambda o: ((o >> 2) & 15) * 16 + (o >> 6) * 4 + (o & 3)),
        landed,
    )
    return (received.reshape(activations.shape), weight_grads.transpose(1, 0, 2)[None])


def solution(mesh):
    in_specs = (
        P("dp", "section", "mp", None, None),
        P("dp", "section", "mp", None, None),
        P("section", None, None, None),
    )
    out_specs = (P("dp", "section", "mp", None, None), P("section", "dp", "mp", None))

    return jax.shard_map(
        per_device, mesh=mesh, in_specs=in_specs, out_specs=out_specs, check_vma=False
    )
```

```python
import jax
import jax.numpy as jnp
import numpy as np
from jax import lax
from jax.experimental import pallas as pl
from jax.experimental.pallas import tpu as pltpu
from jax.sharding import PartitionSpec as P


HEAD_DIM = 64
EPS = 1e-05
F32 = jnp.float32
BF16 = jnp.bfloat16
LANES = 128
ROWS = 4
COLS = 4
CELL = ROWS * COLS
GROUP = 16
BLOCK = GROUP * CELL
NX = 4
PAD = 8
VMEM = pl.BlockSpec(memory_space=pltpu.VMEM)
SMEM = pl.BlockSpec(memory_space=pltpu.SMEM)


def dot(a, b, dims=((1,), (0,))):
    return lax.dot_general(a, b, (dims, ((), ())), preferred_element_type=F32)


def selection(size, source_of):
    out = lax.broadcasted_iota(jnp.int32, (size, size), 0)
    source = lax.broadcasted_iota(jnp.int32, (size, size), 1)
    return jnp.where(source_of(out) == source, 1.0, 0.0).astype(BF16)


def table(rows, columns, source_of):
    matrix = np.zeros((rows, columns), np.float32)
    for o in range(rows):
        if source_of(o) >= 0:
            matrix[o, source_of(o)] = 1.0
    return jnp.asarray(matrix, BF16)


def reorder(matrix, rows):
    return dot(matrix, rows).astype(BF16)


def pack_kernel(_, __, act_ref, grad_ref, out_ref, order_ref):
    @pl.when(pl.program_id(0) == 0)
    def _():
        order_ref[...] = selection(
            BLOCK, lambda o: ((o >> 2) & 3) * 64 + (o >> 4) * 4 + (o & 3)
        )

    for slot, ref in enumerate((act_ref, grad_ref)):
        moved = reorder(order_ref[...], ref[...].reshape(BLOCK, -1)).reshape(GROUP, CELL, -1)
        out_ref[:, slot * CELL : (slot + 1) * CELL] = moved


def attend_kernel(
    replica_ref,
    order_ref,
    back_order_ref,
    in_ref,
    weight_ref,
    back_ref,
    keep_ref,
    give_ref,
    grads_ref,
    delta_ref,
    standard_ref,
    normed_ref,
    attn_ref,
    proj_ref,
):
    peers = in_ref.shape[0]
    groups = peers // GROUP
    width = in_ref.shape[2]
    seqs = peers * ROWS
    span = GROUP * ROWS
    order = order_ref[...]
    for g in range(groups):
        peers_of = slice(g * GROUP, (g + 1) * GROUP)
        acts = dot(order, in_ref[peers_of, :CELL].reshape(BLOCK, width))
        outs = reorder(order, in_ref[peers_of, CELL : 2 * CELL].reshape(BLOCK, width))
        for j in range(COLS):
            to = slice(j * seqs + g * span, j * seqs + (g + 1) * span)
            standard_ref[to] = acts[j * span : (j + 1) * span]
            delta_ref[to] = outs[j * span : (j + 1) * span]
    values = standard_ref[...]
    mean_value = jnp.mean(values, axis=-1, keepdims=True)
    centred = values - mean_value
    inverse = lax.rsqrt(jnp.mean(centred * centred, axis=-1, keepdims=True) + EPS)
    standard = centred * inverse
    standard_ref[...] = standard
    normed = standard.astype(BF16)
    normed_ref[...] = normed
    joint = jnp.concatenate([weight_ref[n] for n in range(3)], axis=1)
    proj_ref[:, : 3 * width] = dot(normed, joint).astype(BF16)
    proj_ref[:, 3 * width :] = dot(delta_ref[...], weight_ref[3]).astype(BF16)

    scaling = HEAD_DIM ** (-0.5)
    low = lax.broadcasted_iota(jnp.int32, (seqs, LANES), 1) < HEAD_DIM

    def apart(pair):
        zero = jnp.zeros_like(pair)
        return jnp.concatenate([jnp.where(low, pair, zero), jnp.where(low, zero, pair)])

    def joined(columns):
        top, bottom = columns[:HEAD_DIM, :seqs], columns[HEAD_DIM:, seqs:]
        return jnp.concatenate([top, bottom]).astype(BF16).T

    def column(j, carry):
        here = pl.ds(pl.multiple_of(j * seqs, seqs), seqs)
        pairs = range(width // LANES)
        loaded = [
            [proj_ref[here, n * width + p * LANES : n * width + (p + 1) * LANES] for n in range(4)]
            for p in pairs
        ]
        split = [(apart(query), apart(delta)) for query, _, _, delta in loaded]
        scores = [dot(loaded[p][1], split[p][0], ((1,), (1,))) * scaling for p in pairs]
        dprobs = [dot(loaded[p][2], split[p][1], ((1,), (1,))) for p in pairs]
        for p in pairs:
            _, key, value, _ = loaded[p]
            queries, deltas = split[p]
            exponent = jnp.exp(scores[p] - jnp.max(scores[p], axis=0, keepdims=True))
            probs = exponent * (1.0 / jnp.sum(exponent, axis=0, keepdims=True))
            column_delta = jnp.sum(probs * dprobs[p], axis=0, keepdims=True)
            soft = probs.astype(BF16)
            dscores = (probs * (dprobs[p] - column_delta)).astype(BF16)
            lanes = [slice(n * width + p * LANES, n * width + (p + 1) * LANES) for n in range(3)]
            attn_ref[here, lanes[0]] = joined(dot(value, soft, ((0,), (0,))))
            grads_ref[here, lanes[0]] = joined(dot(key, dscores, ((0,), (0,))) * scaling)
            grads_ref[here, lanes[1]] = (dot(dscores, queries) * scaling).astype(BF16)
            grads_ref[here, lanes[2]] = dot(soft, deltas).astype(BF16)
        return carry

    lax.fori_loop(0, COLS, column, 0, unroll=4)

    grad_in = dot(grads_ref[...], joint, ((1,), (1,)))
    standard = standard_ref[...]
    grad_mean = jnp.mean(grad_in, axis=-1, keepdims=True)
    grad_proj = jnp.mean(grad_in * standard, axis=-1, keepdims=True)
    branch = inverse * (grad_in - grad_mean - standard * grad_proj)
    branch = branch.astype(BF16).astype(F32)
    input_grad = (delta_ref[...].astype(F32) + branch).astype(BF16)
    order = back_order_ref[...]
    for g in range(groups):
        rows = jnp.concatenate(
            [input_grad[j * seqs + g * span : j * seqs + (g + 1) * span] for j in range(COLS)]
        )
        back_ref[g * GROUP : (g + 1) * GROUP] = reorder(order, rows).reshape(GROUP, CELL, width)

    first = replica_ref[0] == 0
    term = dot(normed_ref[...], grads_ref[...], ((0,), (0,)))
    terms = [term[:, n * width : (n + 1) * width] for n in range(3)]
    terms.append(dot(delta_ref[...], attn_ref[...], ((0,), (0,))))
    for m in range(2):
        keep_ref[m] = jnp.where(first, terms[m], terms[m + 2])
        give_ref[m] = jnp.where(first, terms[m + 2], terms[m]).astype(BF16)


def spread_kernel(order_ref, keep_ref, got_ref, out_ref):
    quarters = out_ref.shape[0]
    block = order_ref.shape[0] // 2
    size = 2 * block // quarters
    for g in range(keep_ref.shape[1] // block):
        here = slice(g * block, (g + 1) * block)
        rows = [(keep_ref[m, here] + got_ref[m, here].astype(F32)).astype(BF16) for m in range(2)]
        moved = reorder(order_ref[...], jnp.concatenate(rows))
        for q in range(quarters):
            out_ref[q, g * size : (g + 1) * size] = moved[q * size : (q + 1) * size]


def collect_kernel(order_ref, parts_ref, out_ref):
    total = jnp.sum(parts_ref[...].astype(F32), axis=0).astype(BF16)
    out_ref[...] = reorder(order_ref[...], total).reshape(out_ref.shape)


def leave_kernel(last_ref, back_ref, cells_ref, out_ref):
    back = back_ref[...]
    out_ref[:, :CELL] = jnp.where(last_ref[0] == 1, jnp.zeros_like(back), back)
    out_ref[:, CELL:] = cells_ref[...]


def final_kernel(order_ref, in_ref, received_ref, grads_ref):
    peers, _, width = in_ref.shape
    groups = peers // GROUP
    residues = peers * COLS
    span = GROUP * COLS
    order = order_ref[...]
    for g in range(groups):
        rows = in_ref[g * GROUP : (g + 1) * GROUP, :CELL].reshape(BLOCK, width)
        moved = reorder(order, rows)
        for i in range(ROWS):
            to = slice(i * residues + g * span, i * residues + (g + 1) * span)
            received_ref[to] = moved[i * span : (i + 1) * span]
    parts = in_ref[:, CELL:].astype(F32)
    quarters = NX
    parts = jnp.sum(parts.reshape(quarters, peers // quarters, PAD, width), axis=1)
    piece = grads_ref.shape[0] // quarters
    for q in range(quarters):
        for u in range(piece):
            grads_ref[q * piece + u] = parts[q, 2 * u : 2 * u + 2]


def shape(dims, dtype=BF16):
    return jax.ShapeDtypeStruct(dims, dtype)


def call(kernel, in_specs, out_shape, scratch=(), cost=(1e8, 1e6)):
    return pl.pallas_call(
        kernel,
        in_specs=in_specs,
        out_specs=jax.tree.map(lambda _: VMEM, out_shape),
        out_shape=out_shape,
        scratch_shapes=scratch,
        compiler_params=pltpu.CompilerParams(vmem_limit_bytes=14 * 1024 * 1024),
        cost_estimate=pl.CostEstimate(
            flops=int(cost[0]), bytes_accessed=int(cost[1]), transcendentals=0
        ),
    )


def exchange(array, groups=None):
    return lax.all_to_all(
        array, "mp", split_axis=0, concat_axis=0, axis_index_groups=groups, tiled=True
    )


def per_device(activations, out_grads, layer_weights):
    rows, residues, width = activations.shape[2:]
    peers = lax.axis_size("mp")
    tokens = rows * residues
    part = width // peers
    replica = lax.axis_index("dp").astype(jnp.int32).reshape(1)
    last = lax.axis_index("section") == lax.axis_size("section") - 1
    last = last.astype(jnp.int32).reshape(1)
    groups = peers // GROUP
    span = GROUP * COLS
    taken = pl.BlockSpec((rows, 1, span, width), lambda g: (0, g, 0, 0))
    packed = pl.pallas_call(
        pack_kernel,
        grid=(groups,),
        in_specs=[SMEM] * 2 + [taken] * 2,
        out_specs=pl.BlockSpec((GROUP, 2 * CELL, width), lambda g: (g, 0, 0)),
        out_shape=shape((peers, 2 * CELL, width)),
        scratch_shapes=[pltpu.VMEM((BLOCK, BLOCK), BF16)],
        compiler_params=pltpu.CompilerParams(vmem_limit_bytes=56 * 1024 * 1024),
    )(
        replica,
        last,
        activations.reshape(rows, groups, span, width),
        out_grads.reshape(rows, groups, span, width),
    )
    arrived = exchange(packed)
    weights = layer_weights[0]
    back, keep, give = call(
        attend_kernel,
        [SMEM] + [VMEM] * 4,
        (
            shape((peers, CELL, width)),
            shape((2, width, width), F32),
            shape((2, width, width)),
        ),
        [
            pltpu.VMEM((tokens, 3 * width), BF16),
            pltpu.VMEM((tokens, width), BF16),
            pltpu.VMEM((tokens, width), F32),
            pltpu.VMEM((tokens, width), BF16),
            pltpu.VMEM((tokens, width), BF16),
            pltpu.VMEM((tokens, 4 * width), BF16),
        ],
        cost=(4e9, 9e6),
    )(
        replica,
        table(BLOCK, BLOCK, lambda o: ((o >> 2) & 15) * 16 + (o & 3) * 4 + (o >> 6)),
        table(BLOCK, BLOCK, lambda o: (o & 3) * 64 + (o >> 4) * 4 + ((o >> 2) & 3)),
        arrived,
        weights,
    )
    got = lax.ppermute(give, "dp", [(0, 1), (1, 0)])
    sections = lax.axis_size("section")
    back = lax.ppermute(back, "section", [(i, (i - 1) % sections) for i in range(sections)])
    piece = part // NX

    def spread_from(o):
        quarter, rest = divmod(o, 16 * piece)
        device, inside = divmod(rest, 2 * piece)
        return (inside & 1) * 8 * part + device * part + quarter * piece + (inside >> 1)

    spread = call(
        spread_kernel, [VMEM] * 3, shape((NX, 2 * width // NX, width)), cost=(1e9, 3e6)
    )(table(16 * part, 16 * part, spread_from), keep, got)
    ny = peers // NX
    groups = [[x * ny + y for x in range(NX)] for y in range(ny)]
    parts = exchange(spread, groups)
    cell = 2 * piece
    order = table(
        peers * PAD, peers * cell, lambda o: (o >> 3) * cell + (o & 7) if (o & 7) < cell else -1
    )
    cells = call(collect_kernel, [VMEM] * 2, shape((peers, PAD, width)))(order, parts)
    leaving = call(leave_kernel, [SMEM] + [VMEM] * 2, shape((peers, CELL + PAD, width)))(
        last, back, cells
    )
    landed = exchange(leaving)
    received, weight_grads = call(
        final_kernel, [VMEM] * 2, (shape((tokens, width)), shape((part, 2, width), F32))
    )(
        table(BLOCK, BLOCK, lambda o: ((o >> 2) & 15) * 16 + (o >> 6) * 4 + (o & 3)),
        landed,
    )
    return (received.reshape(activations.shape), weight_grads.transpose(1, 0, 2)[None])


def solution(mesh):
    in_specs = (
        P("dp", "section", "mp", None, None),
        P("dp", "section", "mp", None, None),
        P("section", None, None, None),
    )
    out_specs = (P("dp", "section", "mp", None, None), P("section", "dp", "mp", None))

    return jax.shard_map(
        per_device, mesh=mesh, in_specs=in_specs, out_specs=out_specs, check_vma=False
    )
```

```python
import jax
import jax.numpy as jnp
import numpy as np
from jax import lax
from jax.experimental import pallas as pl
from jax.experimental.pallas import tpu as pltpu
from jax.sharding import PartitionSpec as P


HEAD_DIM = 64
EPS = 1e-05
F32 = jnp.float32
BF16 = jnp.bfloat16
LANES = 128
ROWS = 4
COLS = 4
CELL = ROWS * COLS
GROUP = 16
BLOCK = GROUP * CELL
NX = 4
NY = 8
PAD = 8
VMEM = pl.BlockSpec(memory_space=pltpu.VMEM)
SMEM = pl.BlockSpec(memory_space=pltpu.SMEM)


def dot(a, b, dims=((1,), (0,))):
    return lax.dot_general(a, b, (dims, ((), ())), preferred_element_type=F32)


def selection(size, source_of):
    out = lax.broadcasted_iota(jnp.int32, (size, size), 0)
    source = lax.broadcasted_iota(jnp.int32, (size, size), 1)
    return jnp.where(source_of(out) == source, 1.0, 0.0).astype(BF16)


def table(rows, columns, source_of):
    matrix = np.zeros((rows, columns), np.float32)
    for o in range(rows):
        if source_of(o) >= 0:
            matrix[o, source_of(o)] = 1.0
    return jnp.asarray(matrix, BF16)


def reorder(matrix, rows):
    return dot(matrix, rows).astype(BF16)


def pack_kernel(_, act_ref, grad_ref, out_ref, order_ref):
    @pl.when(pl.program_id(0) == 0)
    def _():
        order_ref[...] = selection(
            BLOCK, lambda o: ((o >> 2) & 3) * 64 + (o >> 4) * 4 + (o & 3)
        )

    for slot, ref in enumerate((act_ref, grad_ref)):
        moved = reorder(order_ref[...], ref[...].reshape(BLOCK, -1)).reshape(GROUP, CELL, -1)
        out_ref[:, slot * CELL : (slot + 1) * CELL] = moved


def attend_kernel(
    replica_ref,
    order_ref,
    back_order_ref,
    in_ref,
    weight_ref,
    back_ref,
    keep_ref,
    give_ref,
    grads_ref,
    delta_ref,
    standard_ref,
    normed_ref,
    attn_ref,
    proj_ref,
):
    peers = in_ref.shape[0]
    groups = peers // GROUP
    width = in_ref.shape[2]
    seqs = peers * ROWS
    span = GROUP * ROWS
    order = order_ref[...]
    for g in range(groups):
        peers_of = slice(g * GROUP, (g + 1) * GROUP)
        acts = dot(order, in_ref[peers_of, :CELL].reshape(BLOCK, width))
        outs = reorder(order, in_ref[peers_of, CELL : 2 * CELL].reshape(BLOCK, width))
        for j in range(COLS):
            to = slice(j * seqs + g * span, j * seqs + (g + 1) * span)
            standard_ref[to] = acts[j * span : (j + 1) * span]
            delta_ref[to] = outs[j * span : (j + 1) * span]
    values = standard_ref[...]
    mean_value = jnp.mean(values, axis=-1, keepdims=True)
    centred = values - mean_value
    inverse = lax.rsqrt(jnp.mean(centred * centred, axis=-1, keepdims=True) + EPS)
    standard = centred * inverse
    standard_ref[...] = standard
    normed = standard.astype(BF16)
    normed_ref[...] = normed
    joint = jnp.concatenate([weight_ref[n] for n in range(3)], axis=1)
    proj_ref[:, : 3 * width] = dot(normed, joint).astype(BF16)
    proj_ref[:, 3 * width :] = dot(delta_ref[...], weight_ref[3]).astype(BF16)

    scaling = HEAD_DIM ** (-0.5)
    low = lax.broadcasted_iota(jnp.int32, (seqs, LANES), 1) < HEAD_DIM

    def apart(pair):
        zero = jnp.zeros_like(pair)
        return jnp.concatenate([jnp.where(low, pair, zero), jnp.where(low, zero, pair)])

    def joined(columns):
        top, bottom = columns[:HEAD_DIM, :seqs], columns[HEAD_DIM:, seqs:]
        return jnp.concatenate([top, bottom]).astype(BF16).T

    def column(j, carry):
        here = pl.ds(pl.multiple_of(j * seqs, seqs), seqs)
        pairs = range(width // LANES)
        loaded = [
            [proj_ref[here, n * width + p * LANES : n * width + (p + 1) * LANES] for n in range(4)]
            for p in pairs
        ]
        split = [(apart(query), apart(delta)) for query, _, _, delta in loaded]
        scores = [dot(loaded[p][1], split[p][0], ((1,), (1,))) * scaling for p in pairs]
        dprobs = [dot(loaded[p][2], split[p][1], ((1,), (1,))) for p in pairs]
        for p in pairs:
            _, key, value, _ = loaded[p]
            queries, deltas = split[p]
            exponent = jnp.exp(scores[p] - jnp.max(scores[p], axis=0, keepdims=True))
            probs = exponent * (1.0 / jnp.sum(exponent, axis=0, keepdims=True))
            column_delta = jnp.sum(probs * dprobs[p], axis=0, keepdims=True)
            soft = probs.astype(BF16)
            dscores = (probs * (dprobs[p] - column_delta)).astype(BF16)
            lanes = [slice(n * width + p * LANES, n * width + (p + 1) * LANES) for n in range(3)]
            attn_ref[here, lanes[0]] = joined(dot(value, soft, ((0,), (0,))))
            grads_ref[here, lanes[0]] = joined(dot(key, dscores, ((0,), (0,))) * scaling)
            grads_ref[here, lanes[1]] = (dot(dscores, queries) * scaling).astype(BF16)
            grads_ref[here, lanes[2]] = dot(soft, deltas).astype(BF16)
        return carry

    lax.fori_loop(0, COLS, column, 0, unroll=4)

    grad_in = dot(grads_ref[...], joint, ((1,), (1,)))
    standard = standard_ref[...]
    grad_mean = jnp.mean(grad_in, axis=-1, keepdims=True)
    grad_proj = jnp.mean(grad_in * standard, axis=-1, keepdims=True)
    branch = inverse * (grad_in - grad_mean - standard * grad_proj)
    branch = branch.astype(BF16).astype(F32)
    input_grad = (delta_ref[...].astype(F32) + branch).astype(BF16)
    order = back_order_ref[...]
    for g in range(groups):
        rows = jnp.concatenate(
            [input_grad[j * seqs + g * span : j * seqs + (g + 1) * span] for j in range(COLS)]
        )
        back_ref[g * GROUP : (g + 1) * GROUP] = reorder(order, rows).reshape(GROUP, CELL, width)

    first = replica_ref[0] == 0
    term = dot(normed_ref[...], grads_ref[...], ((0,), (0,)))
    terms = [term[:, n * width : (n + 1) * width] for n in range(3)]
    terms.append(dot(delta_ref[...], attn_ref[...], ((0,), (0,))))
    for m in range(2):
        keep_ref[m] = jnp.where(first, terms[m], terms[m + 2])
        give_ref[m] = jnp.where(first, terms[m + 2], terms[m]).astype(BF16)


def spread_kernel(order_ref, keep_ref, got_ref, out_ref):
    quarters = out_ref.shape[0]
    block = order_ref.shape[0] // 2
    size = 2 * block // quarters
    for g in range(keep_ref.shape[1] // block):
        here = slice(g * block, (g + 1) * block)
        rows = [(keep_ref[m, here] + got_ref[m, here].astype(F32)).astype(BF16) for m in range(2)]
        moved = reorder(order_ref[...], jnp.concatenate(rows))
        for q in range(quarters):
            out_ref[q, g * size : (g + 1) * size] = moved[q * size : (q + 1) * size]


def collect_kernel(order_ref, parts_ref, out_ref):
    total = jnp.sum(parts_ref[...].astype(F32), axis=0).astype(BF16)
    out_ref[...] = reorder(order_ref[...], total).reshape(out_ref.shape)


def leave_kernel(back_ref, cells_ref, out_ref):
    out_ref[:, :CELL] = back_ref[...]
    out_ref[:, CELL:] = cells_ref[...]


def final_kernel(order_ref, in_ref, received_ref, grads_ref):
    peers, _, width = in_ref.shape
    moved = reorder(order_ref[...], in_ref[:, :CELL].reshape(BLOCK, width))
    received_ref[...] = moved.reshape(received_ref.shape)
    parts = in_ref[:, CELL:].astype(F32)
    parts = jnp.sum(parts.reshape(peers // NY, NY, PAD, width), axis=1)
    piece = grads_ref.shape[0] * NY // peers
    for q in range(peers // NY):
        for u in range(piece):
            grads_ref[q * piece + u] = parts[q, 2 * u : 2 * u + 2]


def shape(dims, dtype=BF16):
    return jax.ShapeDtypeStruct(dims, dtype)


def call(kernel, in_specs, out_shape, scratch=(), cost=(1e8, 1e6)):
    return pl.pallas_call(
        kernel,
        in_specs=in_specs,
        out_specs=jax.tree.map(lambda _: VMEM, out_shape),
        out_shape=out_shape,
        scratch_shapes=scratch,
        compiler_params=pltpu.CompilerParams(vmem_limit_bytes=14 * 1024 * 1024),
        cost_estimate=pl.CostEstimate(
            flops=int(cost[0]), bytes_accessed=int(cost[1]), transcendentals=0
        ),
    )


def exchange(array, groups=None):
    return lax.all_to_all(
        array, "mp", split_axis=0, concat_axis=0, axis_index_groups=groups, tiled=True
    )


def per_device(activations, out_grads, layer_weights):
    rows, residues, width = activations.shape[2:]
    peers = lax.axis_size("mp")
    tokens = rows * residues
    part = width // peers
    replica = lax.axis_index("dp").astype(jnp.int32).reshape(1)
    groups = peers // GROUP
    span = GROUP * COLS
    taken = pl.BlockSpec((rows, 1, span, width), lambda g: (0, g, 0, 0))
    packed = pl.pallas_call(
        pack_kernel,
        grid=(groups,),
        in_specs=[SMEM] + [taken] * 2,
        out_specs=pl.BlockSpec((GROUP, 2 * CELL, width), lambda g: (g, 0, 0)),
        out_shape=shape((peers, 2 * CELL, width)),
        scratch_shapes=[pltpu.VMEM((BLOCK, BLOCK), BF16)],
        compiler_params=pltpu.CompilerParams(vmem_limit_bytes=56 * 1024 * 1024),
    )(
        replica,
        activations.reshape(rows, groups, span, width),
        out_grads.reshape(rows, groups, span, width),
    )
    arrived = exchange(packed)
    weights = layer_weights[0]
    back, keep, give = call(
        attend_kernel,
        [SMEM] + [VMEM] * 4,
        (
            shape((peers, CELL, width)),
            shape((2, width, width), F32),
            shape((2, width, width)),
        ),
        [
            pltpu.VMEM((tokens, 3 * width), BF16),
            pltpu.VMEM((tokens, width), BF16),
            pltpu.VMEM((tokens, width), F32),
            pltpu.VMEM((tokens, width), BF16),
            pltpu.VMEM((tokens, width), BF16),
            pltpu.VMEM((tokens, 4 * width), BF16),
        ],
        cost=(4e9, 9e6),
    )(
        replica,
        table(BLOCK, BLOCK, lambda o: ((o >> 2) & 15) * 16 + (o & 3) * 4 + (o >> 6)),
        table(BLOCK, BLOCK, lambda o: (o & 3) * 64 + (o >> 4) * 4 + ((o >> 2) & 3)),
        arrived,
        weights,
    )
    got = lax.ppermute(give, "dp", [(0, 1), (1, 0)])
    sections = lax.axis_size("section")
    back = lax.ppermute(back, "section", [(i + 1, i) for i in range(sections - 1)])
    piece = part // NX

    def spread_from(o):
        quarter, rest = divmod(o, 16 * piece)
        device, inside = divmod(rest, 2 * piece)
        return (inside & 1) * 8 * part + device * part + quarter * piece + (inside >> 1)

    spread = call(
        spread_kernel, [VMEM] * 3, shape((NX, 2 * width // NX, width)), cost=(1e9, 3e6)
    )(table(16 * part, 16 * part, spread_from), keep, got)
    ny = peers // NX
    groups = [[x * ny + y for x in range(NX)] for y in range(ny)]
    parts = exchange(spread, groups)
    cell = 2 * piece
    order = table(
        peers * PAD, peers * cell, lambda o: (o >> 3) * cell + (o & 7) if (o & 7) < cell else -1
    )
    cells = call(collect_kernel, [VMEM] * 2, shape((peers, PAD, width)))(order, parts)
    leaving = call(leave_kernel, [VMEM] * 2, shape((peers, CELL + PAD, width)))(back, cells)
    landed = exchange(leaving)
    order = table(BLOCK, BLOCK, lambda o: ((o >> 2) & 15) * 16 + (o >> 6) * 4 + (o & 3))
    received, weight_grads = pl.pallas_call(
        final_kernel,
        grid=(peers // GROUP,),
        in_specs=[
            pl.BlockSpec((BLOCK, BLOCK), lambda g: (0, 0)),
            pl.BlockSpec((GROUP, CELL + PAD, width), lambda g: (g, 0, 0)),
        ],
        out_specs=(taken, pl.BlockSpec((part * GROUP // peers, 2, width), lambda g: (g, 0, 0))),
        out_shape=(shape((rows, peers // GROUP, span, width)), shape((part, 2, width), F32)),
        compiler_params=pltpu.CompilerParams(vmem_limit_bytes=14 * 1024 * 1024),
    )(order, landed)
    return (received.reshape(activations.shape), weight_grads.transpose(1, 0, 2)[None])


def solution(mesh):
    in_specs = (
        P("dp", "section", "mp", None, None),
        P("dp", "section", "mp", None, None),
        P("section", None, None, None),
    )
    out_specs = (P("dp", "section", "mp", None, None), P("section", "dp", "mp", None))

    return jax.shard_map(
        per_device, mesh=mesh, in_specs=in_specs, out_specs=out_specs, check_vma=False
    )
```
